32 devices in a mesh: section: 4 (over y, x), seq: 8 (over z, core).
Axes of the slice: x: 2, y: 2, z: 4, core: 2. Of those that a mesh axis runs over, the one named last changes fastest.
Arguments:
- tokens: bfloat16 [4096, 2048], P('seq', 'section'), may hold values from -6 to 6
- norm_gain: float32 [2048], replicated, may hold values from 0.25 to 1.75
- w_query: bfloat16 [2048, 2048], P('seq', 'section'), may hold values from -0.3125 to 0.3125
- w_key: bfloat16 [2048, 512], P('seq', 'section'), may hold values from -0.125 to 0.125
- w_value: bfloat16 [2048, 512], P('seq', 'section'), may hold values from -0.125 to 0.125
- w_out: bfloat16 [2048, 2048], P('seq', 'section'), may hold values from -0.25 to 0.25
- router_gate: float32 [4096], P('seq'), may hold values from 0.25 to 1
- chosen_blocks: int32 [8, 1], replicated, may hold values from 0 to 3, as said below
- block_counts: int32 [8], replicated, may hold values from 0 to 1, as said below
Outputs:
- mixed: bfloat16 [4096, 2048], P('seq', 'section')
The draws below stay inside these ranges and needn't reach their ends.
Inputs may be any that keep to these rules, and one draw needn't show every extreme that they name: `chosen_blocks`: in each segment's row the entries name distinct blocks of 128 rows of that segment, in increasing order; only the first block_counts entries are used. `block_counts`: some segment has one chosen block and some segment has none.
All inputs are finite; a program needn't handle non-finite values.
Results may differ from the reference program's by a relative error of at most 0.0034.
Values may be sent and summed in bfloat16 or wider, within the bound.
A program may use at most 64 MiB of HBM per device.

```python
import jax
import jax.numpy as jnp
from jax import lax

D = 2048
HEADS = 16
KV_HEADS = 4
HEAD_DIM = 128
BLOCK = 128
TOK_DEV = 512
CAP = 128
TOKENS = 4096
N_SEQ = 8


def route_plan(key):
    base = jax.random.fold_in(key, 4321)
    first_key, second_key, third_key, fourth_key = jax.random.split(base, 4)
    segment_total = TOKENS // TOK_DEV
    block_total = TOK_DEV // BLOCK
    most_blocks = TOK_DEV // (4 * BLOCK)
    counts = jax.random.randint(first_key, (segment_total,), 0, most_blocks + 1)
    full_at = jax.random.randint(second_key, (), 0, segment_total)
    empty_at = (full_at + 1 + jax.random.randint(third_key, (), 0, segment_total - 1)) % segment_total
    segment_index = jnp.arange(segment_total)
    counts = jnp.where(segment_index == full_at, most_blocks, jnp.where(segment_index == empty_at, 0, counts))
    ranking = jax.random.randint(fourth_key, (segment_total, block_total), 0, 1 << 20) * block_total + jnp.arange(block_total)[None, :]
    ordering = jnp.argsort(ranking, axis=1)[:, :most_blocks]
    blocks = jnp.sort(ordering, axis=1)
    return (blocks.astype(jnp.int32), counts.astype(jnp.int32))


def draw_chosen_blocks(key, part):
    return route_plan(key)[0]


def draw_block_counts(key, part):
    return route_plan(key)[1]


def steps_of(own_key, dims, cuts, smallest, top_value):
    level = 1.0
    for position, parts in cuts:
        steps = jax.random.uniform(jax.random.fold_in(jax.random.fold_in(own_key, 6), position), (parts,), jnp.float32, smallest / len(cuts), top_value / len(cuts))
        level = level * jnp.repeat(jnp.exp(steps), dims[position] // parts).reshape((-1,) + (1,) * (len(dims) - 1 - position))
    return level


def noise(own_key, shape, scale, bound, pieces=(), held_as=jnp.bfloat16):
    result = jax.random.normal(own_key, shape, jnp.float32) * scale
    if len(pieces) > 0:
        result = steps_of(own_key, shape, pieces, -0.22, 0.18) * result
    return jnp.clip(result, min=-bound, max=bound).astype(held_as)


def setup_inputs(seed: int = 0) -> dict:
    splits = jax.random.split(jax.random.key(seed), 10)
    tokens = noise(splits[0], (TOKENS, D), 1.0, 6.0, ((0, 8), (1, 4)))
    norm_gain = jnp.clip(1.0 + 0.15 * jax.random.normal(splits[1], (D,), jnp.float32), 0.25, 1.75)
    w_query = noise(splits[2], (D, HEADS * HEAD_DIM), (D // 6) ** -0.5, 0.3125, ((0, 8), (1, 4)))
    w_key = noise(splits[3], (D, KV_HEADS * HEAD_DIM), D ** -0.5, 0.125, ((0, 8), (1, 4)))
    w_value = noise(splits[4], (D, KV_HEADS * HEAD_DIM), D ** -0.5, 0.125, ((0, 8), (1, 4)))
    w_out = noise(splits[5], (HEADS * HEAD_DIM, D), (HEADS * HEAD_DIM // 4) ** -0.5, 0.25, ((0, 8), (1, 4)))
    router_gate = jnp.clip(0.25 + 0.75 * jax.random.uniform(splits[6], (TOKENS,), jnp.float32) ** steps_of(splits[6], (TOKENS,), ((0, 8),), -0.2, 0.2), 0.25, 1.0)
    chosen_blocks = draw_chosen_blocks(jax.random.fold_in(splits[9], 71), 0)
    block_counts = draw_block_counts(jax.random.fold_in(splits[9], 71), 0)
    return dict(tokens=tokens, norm_gain=norm_gain, w_query=w_query, w_key=w_key, w_value=w_value, w_out=w_out, router_gate=router_gate, chosen_blocks=chosen_blocks, block_counts=block_counts)


EPSILON = 1e-05

def reference(tokens, norm_gain, w_query, w_key, w_value, w_out, router_gate, chosen_blocks, block_counts):
    slot_index = jnp.arange(CAP, dtype=jnp.int32)
    slot_block = slot_index // BLOCK
    local_rows = jnp.take(chosen_blocks, slot_block, axis=1).astype(jnp.int32) * BLOCK + (slot_index % BLOCK)[None, :]
    segment_first = (jnp.arange(N_SEQ, dtype=jnp.int32) * TOK_DEV)[:, None]
    places = (segment_first + local_rows).reshape(-1)
    live_slots = (slot_block[None, :] < block_counts[:, None]).reshape(-1)
    key_places = jnp.where(live_slots, places, TOKENS)
    picked = jnp.take(tokens, places, axis=0)
    features = picked.astype(jnp.float32)
    normed = (features * lax.rsqrt(lax.optimization_barrier(jnp.mean(features * features, axis=-1, keepdims=True)) + EPSILON) * norm_gain).astype(jnp.bfloat16)
    queries = jnp.dot(normed, w_query, preferred_element_type=jnp.float32).astype(jnp.bfloat16)
    key_rows = jnp.dot(normed, w_key, preferred_element_type=jnp.float32).astype(jnp.bfloat16)
    value_rows = jnp.dot(normed, w_value, preferred_element_type=jnp.float32).astype(jnp.bfloat16)
    repeat_count = HEADS // KV_HEADS
    slots_total = N_SEQ * CAP
    keys_wide = lax.optimization_barrier(key_rows).astype(jnp.float32).reshape(slots_total, KV_HEADS, HEAD_DIM)
    values_wide = lax.optimization_barrier(value_rows).astype(jnp.float32).reshape(slots_total, KV_HEADS, HEAD_DIM)
    queries_wide = lax.optimization_barrier(queries).astype(jnp.float32).reshape(N_SEQ, CAP, KV_HEADS, repeat_count, HEAD_DIM)
    score_scale = HEAD_DIM ** (-0.5)

    def one_segment(packed):
        segment_queries, segment_places, segment_live = packed
        scores = jnp.einsum('qgrd,kgd->grqk', segment_queries, keys_wide) * score_scale
        allowed = key_places[None, :] <= segment_places[:, None]
        weights = jnp.where(allowed[None, None], jnp.exp(scores), 0.0)
        denominators = lax.optimization_barrier(jnp.sum(weights, axis=-1))
        rounded = lax.optimization_barrier(weights.astype(jnp.bfloat16)).astype(jnp.float32)
        summed = jnp.einsum('grqk,kgd->qgrd', rounded, values_wide)
        safe = jnp.where(segment_live[None, None, :], denominators, 1.0)
        return (summed / jnp.transpose(safe, (2, 0, 1))[..., None]).astype(jnp.bfloat16)
    attended = lax.map(one_segment, (queries_wide, places.reshape(N_SEQ, CAP), live_slots.reshape(N_SEQ, CAP)))
    attended = attended.reshape(slots_total, HEADS * HEAD_DIM)
    update = jnp.dot(attended, w_out, preferred_element_type=jnp.float32)
    gate_rows = jnp.take(router_gate, places)
    new_rows = (features + gate_rows[:, None] * update).astype(jnp.bfloat16)
    targets = jnp.where(live_slots, places, TOKENS)
    return tokens.at[targets].set(new_rows, mode='drop')
```

```python
import functools
import math

import jax
import jax.numpy as jnp
from jax import lax
from jax.experimental import pallas as pl
from jax.experimental.pallas import tpu as pltpu
from jax.sharding import PartitionSpec as P

HEADS = 16
KV_HEADS = 4
HEAD_DIM = 128
BLOCK = 128
EPSILON = 1e-05
MESH = pl.DeviceIdType.MESH

KEY, VALUE, QUERY_A, QUERY_B, PANEL, OUT_A, OUT_B = range(7)


def repeat(low, high, body):
    if high - low <= 4:
        for step in range(low, high):
            body(step)
    elif high > low:

        def wrapped(step, carry):
            body(step)
            return carry

        lax.fori_loop(low, high, wrapped, 0)


def kernel(
    seq_count,
    section_count,
    picked_ref,
    gain_ref,
    gate_ref,
    place_ref,
    live_ref,
    key_place_ref,
    wq_in,
    wk_in,
    wv_in,
    wo_in,
    out_ref,
    rows_all,
    normed_ref,
    wk,
    wv,
    wq,
    wo,
    panel,
    queries_ref,
    numer_ref,
    denom_ref,
    heads_all,
    recv,
    send_up,
    send_down,
    send_pair,
    own_sem,
    rows_send,
    rows_recv,
    heads_send,
    heads_recv,
):
    me = lax.axis_index("seq")
    section = lax.axis_index("section")
    line = seq_count // 2
    spot = me // 2
    core = lax.rem(me, 2)
    pair = spot * 2 + 1 - core
    capacity, width = picked_ref.shape
    kv_cols = wk_in.shape[1]
    groups = kv_cols // HEAD_DIM
    ratio = HEADS // KV_HEADS
    half_q = wq_in.shape[1] // 2
    half_o = wo_in.shape[1] // 2
    depth = section_count * width

    def rows_of(block, size):
        return pl.ds(pl.multiple_of(block * size, size), size)

    def full(chunk, block):
        if chunk == KEY:
            return wk.at[rows_of(block, wk_in.shape[0]), :]
        if chunk == VALUE:
            return wv.at[rows_of(block, wv_in.shape[0]), :]
        if chunk in (QUERY_A, QUERY_B):
            return wq.at[chunk - QUERY_A, rows_of(block, wq_in.shape[0]), :]
        if chunk == PANEL:
            return panel.at[rows_of(block, capacity), :]
        return wo.at[chunk - OUT_A, rows_of(block, wo_in.shape[0]), :]

    def own(chunk):
        if chunk == KEY:
            return wk_in
        if chunk == VALUE:
            return wv_in
        if chunk in (QUERY_A, QUERY_B):
            return wq_in.at[:, pl.ds((chunk - QUERY_A) * half_q, half_q)]
        if chunk == PANEL:
            return full(PANEL, me)
        return wo_in.at[:, pl.ds((chunk - OUT_A) * half_o, half_o)]

    def transfer(chunk, source, sems, target, mine):
        block = source * 2 + core
        return pltpu.make_async_remote_copy(
            src_ref=own(chunk) if mine else full(chunk, block),
            dst_ref=full(chunk, block),
            send_sem=sems.at[chunk, source],
            recv_sem=recv.at[chunk, block],
            device_id={"seq": target},
            device_id_type=MESH,
        )

    def await_block(chunk, block):
        pltpu.make_async_remote_copy(
            src_ref=full(chunk, block),
            dst_ref=full(chunk, block),
            send_sem=send_pair.at[chunk, 0],
            recv_sem=recv.at[chunk, block],
            device_id={"seq": pair},
            device_id_type=MESH,
        ).wait_recv()

    def begin(chunk):
        @pl.when(spot + 1 < line)
        def _():
            transfer(chunk, spot, send_up, me + 2, True).start()

        @pl.when(spot > 0)
        def _():
            transfer(chunk, spot, send_down, me - 2, True).start()

        transfer(chunk, spot, send_pair, pair, True).start()

    def relay(chunk, step):
        @pl.when(spot - step >= 0)
        def _():
            source = spot - step
            await_block(chunk, source * 2 + core)

            @pl.when(spot + 1 < line)
            def _():
                transfer(chunk, source, send_up, me + 2, False).start()

            transfer(chunk, source, send_pair, pair, False).start()

        @pl.when(spot + step < line)
        def _():
            source = spot + step
            await_block(chunk, source * 2 + core)

            @pl.when(spot > 0)
            def _():
                transfer(chunk, source, send_down, me - 2, False).start()

            transfer(chunk, source, send_pair, pair, False).start()

    def relay_all(chunks, low, high):
        def body(step):
            for chunk in chunks:
                relay(chunk, step)

        repeat(low, high, body)

    def await_pair(chunk):
        repeat(0, line, lambda source: await_block(chunk, source * 2 + 1 - core))

    def finish_sends(chunk):
        def body(source):
            @pl.when((spot + 1 < line) & (source <= spot))
            def _():
                transfer(chunk, source, send_up, me + 2, False).wait_send()

            @pl.when((spot > 0) & (source >= spot))
            def _():
                transfer(chunk, source, send_down, me - 2, False).wait_send()

            transfer(chunk, source, send_pair, pair, False).wait_send()

        repeat(0, line, body)

    def own_copy(chunk):
        return pltpu.make_async_copy(own(chunk), full(chunk, me), own_sem.at[chunk])

    def spread(source, target, send, receive, offset):
        peer = lax.rem(section + offset, section_count)
        return pltpu.make_async_remote_copy(
            src_ref=source,
            dst_ref=target.at[section],
            send_sem=send.at[offset],
            recv_sem=receive.at[section],
            device_id={"section": peer},
            device_id_type=MESH,
        )

    def await_spread(target, send, receive, offset):
        peer = lax.rem(section + offset, section_count)
        pltpu.make_async_remote_copy(
            src_ref=target.at[peer],
            dst_ref=target.at[peer],
            send_sem=send.at[offset],
            recv_sem=receive.at[peer],
            device_id={"section": peer},
            device_id_type=MESH,
        ).wait_recv()

    barrier = pltpu.get_barrier_semaphore()

    @pl.when(spot + 1 < line)
    def _():
        pl.semaphore_signal(barrier, inc=1, device_id={"seq": me + 2}, device_id_type=MESH)

    @pl.when(spot > 0)
    def _():
        pl.semaphore_signal(barrier, inc=1, device_id={"seq": me - 2}, device_id_type=MESH)

    pl.semaphore_signal(barrier, inc=1, device_id={"seq": pair}, device_id_type=MESH)
    for offset in range(1, section_count):
        peer = lax.rem(section + offset, section_count)
        pl.semaphore_signal(barrier, inc=1, device_id={"section": peer}, device_id_type=MESH)
    neighbours = jnp.where(spot + 1 < line, 1, 0) + jnp.where(spot > 0, 1, 0)
    pl.semaphore_wait(barrier, section_count + neighbours)

    begin(KEY)
    begin(VALUE)
    for offset in range(1, section_count):
        spread(picked_ref, rows_all, rows_send, rows_recv, offset).start()
    for chunk in (KEY, VALUE, QUERY_A, QUERY_B, OUT_A, OUT_B):
        own_copy(chunk).start()
    rows_all[section] = picked_ref[...]
    relay_all((KEY, VALUE), 1, line - 1)
    begin(QUERY_A)
    begin(QUERY_B)
    for offset in range(1, section_count):
        await_spread(rows_all, rows_send, rows_recv, offset)
    square_sum = jnp.zeros((capacity, 1), jnp.float32)
    for part in range(section_count):
        features = rows_all[part].astype(jnp.float32)
        square_sum += jnp.sum(features * features, axis=-1, keepdims=True)
    factor = lax.rsqrt(square_sum / depth + EPSILON)
    for part in range(section_count):
        cols = pl.ds(part * width, width)
        normed_ref[:, cols] = (
            rows_all[part].astype(jnp.float32) * factor * gain_ref[:, cols]
        ).astype(jnp.bfloat16)
    relay_all((KEY, VALUE), max(line - 1, 1), line)
    for chunk in (KEY, VALUE):
        await_pair(chunk)
        own_copy(chunk).wait()
    normed = normed_ref[...]
    my_rows = rows_of(me, capacity)
    panel[my_rows, pl.ds(0, kv_cols)] = jnp.dot(
        normed, wk[...], preferred_element_type=jnp.float32
    ).astype(jnp.bfloat16)
    panel[my_rows, pl.ds(kv_cols, kv_cols)] = jnp.dot(
        normed, wv[...], preferred_element_type=jnp.float32
    ).astype(jnp.bfloat16)
    begin(PANEL)
    relay_all((QUERY_A, QUERY_B, PANEL), 1, line - 1)
    begin(OUT_A)
    begin(OUT_B)
    relay_all((QUERY_A, QUERY_B, PANEL), max(line - 1, 1), line)
    heads_half = half_q // HEAD_DIM
    for half in range(2):
        await_pair(QUERY_A + half)
        own_copy(QUERY_A + half).wait()
        sums = jnp.dot(normed_ref[...], wq[half], preferred_element_type=jnp.float32)
        for head in range(heads_half):
            queries_ref[half * heads_half + head] = sums[
                :, head * HEAD_DIM : (head + 1) * HEAD_DIM
            ].astype(jnp.bfloat16)
    await_pair(PANEL)
    scale = HEAD_DIM ** (-0.5)
    tiles, tile = key_place_ref.shape
    places = jnp.concatenate([place_ref[...]] * ratio, axis=0)
    live = jnp.concatenate([live_ref[...]] * ratio, axis=0)
    for group in range(groups):
        numer_ref[...] = jnp.zeros_like(numer_ref)
        denom_ref[...] = jnp.zeros_like(denom_ref)

        def fold(index):
            rows = pl.ds(index * tile, tile)
            keys = panel[rows, pl.ds(group * HEAD_DIM, HEAD_DIM)]
            values = panel[rows, pl.ds(kv_cols + group * HEAD_DIM, HEAD_DIM)]
            wide = queries_ref[pl.ds(group * ratio, ratio)].reshape(ratio * capacity, HEAD_DIM)
            scores = (
                lax.dot_general(
                    wide, keys, (((1,), (1,)), ((), ())), preferred_element_type=jnp.float32
                )
                * scale
            )
            allowed = key_place_ref[pl.ds(index, 1), :] <= places
            weights = jnp.where(allowed, jnp.exp(scores), 0.0)
            denom_ref[...] += jnp.sum(weights, axis=-1, keepdims=True)
            numer_ref[...] += jnp.dot(
                weights.astype(jnp.bfloat16), values, preferred_element_type=jnp.float32
            )

        repeat(0, tiles, fold)
        safe = jnp.where(live > 0, denom_ref[...], 1.0)
        result = (numer_ref[...] / safe).astype(jnp.bfloat16)
        for head in range(ratio):
            cols = pl.ds((group * ratio + head) * HEAD_DIM, HEAD_DIM)
            heads_all[section, :, cols] = result[head * capacity : (head + 1) * capacity]
    for offset in range(1, section_count):
        spread(heads_all.at[section], heads_all, heads_send, heads_recv, offset).start()
    relay_all((OUT_A, OUT_B), 1, line)
    for offset in range(1, section_count):
        await_spread(heads_all, heads_send, heads_recv, offset)
    head_cols = heads_all.shape[2]
    for half in range(2):
        await_pair(OUT_A + half)
        own_copy(OUT_A + half).wait()
        update = jnp.zeros((capacity, half_o), jnp.float32)
        for part in range(section_count):
            update += jnp.dot(
                heads_all[part],
                wo[half, pl.ds(part * head_cols, head_cols), :],
                preferred_element_type=jnp.float32,
            )
        cols = pl.ds(half * half_o, half_o)
        out_ref[:, cols] = (
            picked_ref[:, cols].astype(jnp.float32) + gate_ref[...] * update
        ).astype(out_ref.dtype)
    for chunk in range(7):
        finish_sends(chunk)
    for offset in range(1, section_count):
        spread(picked_ref, rows_all, rows_send, rows_recv, offset).wait_send()
        spread(heads_all.at[section], heads_all, heads_send, heads_recv, offset).wait_send()


def local(
    tokens, norm_gain, w_query, w_key, w_value, w_out, router_gate, chosen_blocks, block_counts
):
    seq_count = lax.axis_size("seq")
    section_count = lax.axis_size("section")
    me = lax.axis_index("seq")
    tok_rows, width = tokens.shape
    slots = chosen_blocks.shape[1]
    capacity = slots * BLOCK
    beyond = seq_count * tok_rows
    depth = section_count * width
    query_cols = w_query.shape[1]
    kv_cols = w_key.shape[1]
    ratio = HEADS // KV_HEADS
    line = seq_count // 2

    within = jnp.arange(BLOCK, dtype=jnp.int32)
    place_all = (
        jnp.arange(seq_count, dtype=jnp.int32)[:, None, None] * tok_rows
        + chosen_blocks[:, :, None] * BLOCK
        + within[None, None, :]
    )
    live_all = (
        jnp.arange(slots, dtype=jnp.int32)[None, :, None] < block_counts[:, None, None]
    )
    key_place = jnp.where(live_all, place_all, beyond).reshape(-1)
    tile = math.gcd(key_place.shape[0], 512)
    key_place = key_place.reshape(-1, tile)

    my_blocks = lax.dynamic_index_in_dim(chosen_blocks, me, 0, keepdims=False)
    my_count = lax.dynamic_index_in_dim(block_counts, me, 0, keepdims=False)
    starts = [my_blocks[slot] * BLOCK for slot in range(slots)]
    picked = jnp.concatenate(
        [lax.dynamic_slice_in_dim(tokens, start, BLOCK, 0) for start in starts], axis=0
    )
    gates = jnp.concatenate(
        [lax.dynamic_slice_in_dim(router_gate, start, BLOCK, 0) for start in starts], axis=0
    )
    my_places = jnp.concatenate([me * tok_rows + start + within for start in starts])
    my_live = (jnp.arange(capacity, dtype=jnp.int32) // BLOCK < my_count).astype(jnp.int32)

    vmem = pl.BlockSpec(memory_space=pltpu.VMEM)
    anywhere = pl.BlockSpec(memory_space=pl.ANY)
    bf16 = jnp.bfloat16
    dma = pltpu.SemaphoreType.DMA
    new_rows = pl.pallas_call(
        functools.partial(kernel, seq_count, section_count),
        out_shape=jax.ShapeDtypeStruct((capacity, width), tokens.dtype),
        in_specs=[vmem] * 6 + [anywhere] * 4,
        out_specs=vmem,
        scratch_shapes=[
            pltpu.VMEM((section_count, capacity, width), bf16),
            pltpu.VMEM((capacity, depth), bf16),
            pltpu.VMEM((depth, kv_cols), bf16),
            pltpu.VMEM((depth, kv_cols), bf16),
            pltpu.VMEM((2, depth, query_cols // 2), bf16),
            pltpu.VMEM((2, w_out.shape[0] * seq_count, w_out.shape[1] // 2), bf16),
            pltpu.VMEM((seq_count * capacity, 2 * kv_cols), bf16),
            pltpu.VMEM((query_cols // HEAD_DIM, capacity, HEAD_DIM), bf16),
            pltpu.VMEM((ratio * capacity, HEAD_DIM), jnp.float32),
            pltpu.VMEM((ratio * capacity, 1), jnp.float32),
            pltpu.VMEM((section_count, capacity, query_cols), bf16),
            dma((7, seq_count)),
            dma((7, line)),
            dma((7, line)),
            dma((7, line)),
            dma((7,)),
            dma((section_count,)),
            dma((section_count,)),
            dma((section_count,)),
            dma((section_count,)),
        ],
        compiler_params=pltpu.CompilerParams(collective_id=0, has_side_effects=True),
    )(
        picked,
        norm_gain[None, :],
        gates[:, None],
        my_places[:, None],
        my_live[:, None],
        key_place,
        w_query,
        w_key,
        w_value,
        w_out,
    )
    mixed = tokens
    for slot, start in enumerate(starts):
        part = slice(slot * BLOCK, (slot + 1) * BLOCK)
        chosen = jnp.where(slot < my_count, new_rows[part], picked[part])
        mixed = lax.dynamic_update_slice_in_dim(mixed, chosen, start, 0)
    return mixed


def solution(mesh):
    return jax.shard_map(
        local,
        mesh=mesh,
        in_specs=(
            P("seq", "section"),
            P(),
            P("seq", "section"),
            P("seq", "section"),
            P("seq", "section"),
            P("seq", "section"),
            P("seq"),
            P(),
            P(),
        ),
        out_specs=P("seq", "section"),
        check_vma=False,
    )
```

```python
import functools
import math

import jax
import jax.numpy as jnp
from jax import lax
from jax.experimental import pallas as pl
from jax.experimental.pallas import tpu as pltpu
from jax.sharding import PartitionSpec as P

HEADS = 16
KV_HEADS = 4
HEAD_DIM = 128
BLOCK = 128
EPSILON = 1e-05
MESH = pl.DeviceIdType.MESH

KEY, VALUE, QUERY_A, QUERY_B, OUT_A, OUT_B, PANEL, GUEST_PANEL = range(8)


def repeat(low, high, body):
    if high - low <= 4:
        for step in range(low, high):
            body(step)
    elif high > low:

        def wrapped(step, carry):
            body(step)
            return carry

        lax.fori_loop(low, high, wrapped, 0)


def kernel(
    seq_count,
    section_count,
    picked_ref,
    gain_ref,
    gate_ref,
    key_slot_ref,
    wq_in,
    wk_in,
    wv_in,
    wo_in,
    out_ref,
    rows_all,
    gate_rows,
    normed_ref,
    wk,
    wv,
    wq,
    wo,
    panel,
    queries_ref,
    numer_ref,
    denom_ref,
    heads_all,
    results,
    returned,
    recv,
    send_line,
    send_pair,
    own_sem,
    rows_send,
    rows_recv,
    heads_send,
    heads_recv,
    guest_send,
    guest_recv,
    back_send,
    back_recv,
):
    me = lax.axis_index("seq")
    section = lax.axis_index("section")
    line = seq_count // 2
    spot = me // 2
    core = lax.rem(me, 2)
    pair = spot * 2 + 1 - core
    slots = gate_ref.shape[0]
    capacity, width = out_ref.shape
    kv_cols = wk_in.shape[1]
    groups = kv_cols // HEAD_DIM
    ratio = HEADS // KV_HEADS
    half_q = wq_in.shape[1] // 2
    half_o = wo_in.shape[1] // 2
    depth = section_count * width
    first, last = 1, line - 2
    active = (spot >= first) & (spot <= last)
    has_guest = (spot == first) | (spot == last)
    near = jnp.where(spot * 2 < line, 1, -1)
    guest_spot = spot - near
    guest = me - 2 * near
    host = me + 2 * near

    def rows_of(block, size):
        return pl.ds(pl.multiple_of(block * size, size), size)

    def full(chunk, block):
        if chunk == KEY:
            return wk.at[rows_of(block, wk_in.shape[0]), :]
        if chunk == VALUE:
            return wv.at[rows_of(block, wv_in.shape[0]), :]
        if chunk in (QUERY_A, QUERY_B):
            return wq.at[chunk - QUERY_A, rows_of(block, wq_in.shape[0]), :]
        if chunk in (PANEL, GUEST_PANEL):
            return panel.at[rows_of(block, capacity), :]
        return wo.at[chunk - OUT_A, rows_of(block, wo_in.shape[0]), :]

    def own(chunk):
        if chunk == KEY:
            return wk_in
        if chunk == VALUE:
            return wv_in
        if chunk in (QUERY_A, QUERY_B):
            return wq_in.at[:, pl.ds((chunk - QUERY_A) * half_q, half_q)]
        return wo_in.at[:, pl.ds((chunk - OUT_A) * half_o, half_o)]

    def transfer(chunk, block, send_sem, target, mine):
        return pltpu.make_async_remote_copy(
            src_ref=own(chunk) if mine else full(chunk, block),
            dst_ref=full(chunk, block),
            send_sem=send_sem,
            recv_sem=recv.at[min(chunk, PANEL), block],
            device_id={"seq": target},
            device_id_type=MESH,
        )

    def along(chunk, source, sign, mine):
        way = (1 - sign) // 2
        return transfer(
            chunk, source * 2 + core, send_line.at[way, min(chunk, PANEL), source], me + 2 * sign, mine
        )

    def across(chunk, source, mine):
        return transfer(
            chunk, source * 2 + core, send_pair.at[min(chunk, PANEL), source], pair, mine
        )

    def onward(sign):
        return (spot + sign >= first) & (spot + sign <= last)

    def begin(chunk, source):
        mine = chunk < PANEL
        for sign in (1, -1):

            @pl.when(onward(sign))
            def _():
                along(chunk, source, sign, mine).start()

        @pl.when(active)
        def _():
            across(chunk, source, mine).start()

    def relay(chunk, step, sign):
        source = spot - sign * step
        low, high = (first, last) if chunk >= PANEL else (0, line - 1)
        valid = active & (source >= low) & (source <= high)
        if chunk == GUEST_PANEL:
            valid = active & (source == jnp.where(sign > 0, first, last))
            source = source - sign

        @pl.when(valid)
        def _():
            across(chunk, source, False).wait_recv()

            @pl.when(onward(sign))
            def _():
                along(chunk, source, sign, False).start()

            across(chunk, source, False).start()

    def relay_all(chunks, low, high, sides=(1, -1)):
        def body(step):
            for side in sides:
                for chunk in chunks:
                    relay(chunk, step, side * near)

        repeat(low, high, body)

    def await_pair(chunk):
        def body(source):
            transfer(
                chunk, source * 2 + 1 - core, send_pair.at[chunk, source], pair, False
            ).wait_recv()

        repeat(0, line, body)

    def finish_sends(chunk):
        def body(source):
            for sign in (1, -1):
                origin = jnp.clip(source, first, last) if chunk == PANEL else source

                @pl.when(onward(sign) & (origin * sign <= spot * sign))
                def _():
                    along(chunk, source, sign, False).wait_send()

            @pl.when(active)
            def _():
                across(chunk, source, False).wait_send()

        if chunk == PANEL:

            def guarded(source):
                pl.when(active)(lambda: body(source))

            repeat(0, line, guarded)
        else:
            repeat(0, line, body)

    def own_copy(chunk):
        return pltpu.make_async_copy(own(chunk), full(chunk, me), own_sem.at[chunk])

    def spread(buffer, send, receive, who, offset):
        peer = lax.rem(section + offset, section_count)
        from_input = buffer is rows_all and who == 0
        return pltpu.make_async_remote_copy(
            src_ref=picked_ref if from_input else buffer.at[section, who],
            dst_ref=buffer.at[section, who],
            send_sem=send.at[who, offset],
            recv_sem=receive.at[who, section],
            device_id={"section": peer},
            device_id_type=MESH,
        )

    def await_spread(buffer, send, receive, who):
        for offset in range(1, section_count):
            peer = lax.rem(section + offset, section_count)
            pltpu.make_async_remote_copy(
                src_ref=buffer.at[peer, who],
                dst_ref=buffer.at[peer, who],
                send_sem=send.at[who, offset],
                recv_sem=receive.at[who, peer],
                device_id={"section": peer},
                device_id_type=MESH,
            ).wait_recv()

    def to_host():
        return (
            pltpu.make_async_remote_copy(
                src_ref=picked_ref,
                dst_ref=rows_all.at[section, 1],
                send_sem=guest_send.at[0],
                recv_sem=guest_recv.at[0],
                device_id={"seq": host},
                device_id_type=MESH,
            ),
            pltpu.make_async_remote_copy(
                src_ref=gate_ref,
                dst_ref=gate_rows.at[1],
                send_sem=guest_send.at[1],
                recv_sem=guest_recv.at[1],
                device_id={"seq": host},
                device_id_type=MESH,
            ),
        )

    def give_back(half, target):
        return pltpu.make_async_remote_copy(
            src_ref=results.at[half],
            dst_ref=returned.at[half],
            send_sem=back_send.at[half],
            recv_sem=back_recv.at[half],
            device_id={"seq": target},
            device_id_type=MESH,
        )

    rows_all[section, 0] = picked_ref[...]
    gate_rows[0] = gate_ref[...]

    barrier = pltpu.get_barrier_semaphore()

    @pl.when(spot + 1 < line)
    def _():
        pl.semaphore_signal(barrier, inc=1, device_id={"seq": me + 2}, device_id_type=MESH)

    @pl.when(spot > 0)
    def _():
        pl.semaphore_signal(barrier, inc=1, device_id={"seq": me - 2}, device_id_type=MESH)

    pl.semaphore_signal(barrier, inc=1, device_id={"seq": pair}, device_id_type=MESH)
    for offset in range(1, section_count):
        peer = lax.rem(section + offset, section_count)
        pl.semaphore_signal(barrier, inc=1, device_id={"section": peer}, device_id_type=MESH)
    neighbours = jnp.where(spot + 1 < line, 1, 0) + jnp.where(spot > 0, 1, 0)
    pl.semaphore_wait(barrier, section_count + neighbours)

    weights_chunks = (KEY, VALUE, QUERY_A, QUERY_B, OUT_A, OUT_B)

    @pl.when(jnp.logical_not(active))
    def _():
        for copy in to_host():
            copy.start()
        for chunk in weights_chunks:
            begin(chunk, spot)

    def gate_column(who):
        wide = gate_rows[who]
        square = lax.broadcasted_iota(jnp.int32, (BLOCK, BLOCK), 0) == lax.broadcasted_iota(
            jnp.int32, (BLOCK, BLOCK), 1
        )
        return jnp.concatenate(
            [
                jnp.sum(jnp.where(square, wide[slot : slot + 1, :], 0.0), axis=1, keepdims=True)
                for slot in range(slots)
            ],
            axis=0,
        )

    def normalise(who):
        square_sum = jnp.zeros((capacity, 1), jnp.float32)
        for part in range(section_count):
            features = rows_all[part, who].astype(jnp.float32)
            square_sum += jnp.sum(features * features, axis=-1, keepdims=True)
        factor = lax.rsqrt(square_sum / depth + EPSILON)
        for part in range(section_count):
            cols = pl.ds(part * width, width)
            normed_ref[pl.ds(who * capacity, capacity), cols] = (
                rows_all[part, who].astype(jnp.float32) * factor * gain_ref[:, cols]
            ).astype(jnp.bfloat16)

    def attend(who, owner):
        scale = HEAD_DIM ** (-0.5)
        total = seq_count * capacity
        tile = key_slot_ref.shape[1]
        tall = lax.broadcasted_iota(jnp.int32, (ratio * capacity, 1), 0)
        query_slot = lax.rem(tall, capacity) + owner * capacity
        for group in range(groups):
            numer_ref[...] = jnp.zeros_like(numer_ref)
            denom_ref[...] = jnp.zeros_like(denom_ref)

            def fold(index):
                start = index * tile
                key_slot = key_slot_ref[pl.ds(index, 1), :]
                rows = pl.ds(pl.multiple_of(start, tile), tile)
                keys = panel[rows, pl.ds(group * HEAD_DIM, HEAD_DIM)]
                values = panel[rows, pl.ds(kv_cols + group * HEAD_DIM, HEAD_DIM)]
                wide = queries_ref[who, pl.ds(group * ratio, ratio)].reshape(
                    ratio * capacity, HEAD_DIM
                )
                scores = (
                    lax.dot_general(
                        wide, keys, (((1,), (1,)), ((), ())), preferred_element_type=jnp.float32
                    )
                    * scale
                )
                weights = jnp.where(key_slot <= query_slot, jnp.exp(scores), 0.0)
                denom_ref[...] += jnp.sum(weights, axis=-1, keepdims=True)
                numer_ref[...] += jnp.dot(
                    weights.astype(jnp.bfloat16), values, preferred_element_type=jnp.float32
                )

            repeat(0, total // tile, fold)
            safe = jnp.where(denom_ref[...] > 0, denom_ref[...], 1.0)
            result = (numer_ref[...] / safe).astype(jnp.bfloat16)
            for head in range(ratio):
                cols = pl.ds((group * ratio + head) * HEAD_DIM, HEAD_DIM)
                heads_all[section, who, :, cols] = result[head * capacity : (head + 1) * capacity]

    def finish(who, half):
        update = jnp.zeros((capacity, half_o), jnp.float32)
        head_cols = heads_all.shape[3]
        for part in range(section_count):
            update += jnp.dot(
                heads_all[part, who],
                wo[half, pl.ds(part * head_cols, head_cols), :],
                preferred_element_type=jnp.float32,
            )
        cols = pl.ds(half * half_o, half_o)
        return (
            rows_all[section, who, :, cols].astype(jnp.float32) + gate_column(who) * update
        ).astype(out_ref.dtype)

    @pl.when(active)
    def _():
        begin(KEY, spot)
        begin(VALUE, spot)
        for offset in range(1, section_count):
            spread(rows_all, rows_send, rows_recv, 0, offset).start()

        @pl.when(has_guest)
        def _():
            for copy in to_host():
                copy.wait_recv()
            for offset in range(1, section_count):
                spread(rows_all, rows_send, rows_recv, 1, offset).start()

        for chunk in weights_chunks:
            own_copy(chunk).start()
        relay_all((KEY, VALUE), 1, 2, (1,))
        begin(QUERY_A, spot)
        begin(QUERY_B, spot)
        relay_all((KEY, VALUE), 1, 2, (-1,))
        relay_all((KEY, VALUE), 2, line)
        await_spread(rows_all, rows_send, rows_recv, 0)
        normalise(0)
        relay_all((QUERY_A, QUERY_B), 1, 2, (1,))

        @pl.when(has_guest)
        def _():
            await_spread(rows_all, rows_send, rows_recv, 1)
            normalise(1)

        for chunk in (KEY, VALUE):
            await_pair(chunk)
            own_copy(chunk).wait()
        for position, weight in enumerate((wk, wv)):
            sums = jnp.dot(
                normed_ref[...], weight[...], preferred_element_type=jnp.float32
            ).astype(jnp.bfloat16)
            cols = pl.ds(position * kv_cols, kv_cols)
            panel[rows_of(me, capacity), cols] = sums[:capacity]

            @pl.when(has_guest)
            def _():
                panel[rows_of(guest, capacity), cols] = sums[capacity:]

        begin(PANEL, spot)

        @pl.when(has_guest)
        def _():
            begin(GUEST_PANEL, guest_spot)

        begin(OUT_A, spot)
        begin(OUT_B, spot)
        relay_all((QUERY_A, QUERY_B), 1, 2, (-1,))
        relay_all((QUERY_A, QUERY_B), 2, line)
        relay_all((PANEL, GUEST_PANEL), 1, line)
        relay_all((OUT_A, OUT_B), 1, 2, (1,))
        heads_half = half_q // HEAD_DIM
        for half in range(2):
            await_pair(QUERY_A + half)
            own_copy(QUERY_A + half).wait()
            sums = jnp.dot(
                normed_ref[...], wq[half], preferred_element_type=jnp.float32
            ).astype(jnp.bfloat16)
            for who in range(2):
                for head in range(heads_half):
                    queries_ref[who, half * heads_half + head] = sums[
                        who * capacity : (who + 1) * capacity,
                        head * HEAD_DIM : (head + 1) * HEAD_DIM,
                    ]
        await_pair(PANEL)

        @pl.when(has_guest)
        def _():
            attend(1, guest)
            for offset in range(1, section_count):
                spread(heads_all, heads_send, heads_recv, 1, offset).start()

        attend(0, me)
        for offset in range(1, section_count):
            spread(heads_all, heads_send, heads_recv, 0, offset).start()
        relay_all((OUT_A, OUT_B), 1, 2, (-1,))
        relay_all((OUT_A, OUT_B), 2, line)
        for half in range(2):
            await_pair(OUT_A + half)
            own_copy(OUT_A + half).wait()

        @pl.when(has_guest)
        def _():
            await_spread(heads_all, heads_send, heads_recv, 1)
            for half in range(2):
                results[half] = finish(1, half)
                give_back(half, guest).start()

        await_spread(heads_all, heads_send, heads_recv, 0)
        for half in range(2):
            out_ref[:, pl.ds(half * half_o, half_o)] = finish(0, half)
        for offset in range(1, section_count):
            spread(rows_all, rows_send, rows_recv, 0, offset).wait_send()
            spread(heads_all, heads_send, heads_recv, 0, offset).wait_send()

        @pl.when(has_guest)
        def _():
            for offset in range(1, section_count):
                spread(rows_all, rows_send, rows_recv, 1, offset).wait_send()
                spread(heads_all, heads_send, heads_recv, 1, offset).wait_send()
            for half in range(2):
                give_back(half, guest).wait_send()

    for chunk in weights_chunks + (PANEL,):
        finish_sends(chunk)

    @pl.when(jnp.logical_not(active))
    def _():
        for copy in to_host():
            copy.wait_send()
        for half in range(2):
            give_back(half, host).wait_recv()
            out_ref[:, pl.ds(half * half_o, half_o)] = returned[half]


def pick(
    seq_count, tokens_ref, gate_ref, chosen_ref, count_ref, picked_ref, gates_ref, key_slot_ref, sems
):
    me = lax.axis_index("seq")
    slots = chosen_ref.shape[1]
    tiles, tile = key_slot_ref.shape
    total = tiles * tile

    def rows_copy(slot):
        start = pl.multiple_of(chosen_ref[me, slot] * BLOCK, BLOCK)
        return pltpu.make_async_copy(
            tokens_ref.at[pl.ds(start, BLOCK), :],
            picked_ref.at[pl.ds(slot * BLOCK, BLOCK), :],
            sems.at[slot],
        )

    for slot in range(slots):
        rows_copy(slot).start()
    lane = lax.broadcasted_iota(jnp.int32, (1, tile), 1)

    def fill(index):
        key_slot = lane + index * tile
        for piece in range(tile // BLOCK):
            number = index * (tile // BLOCK) + piece
            live = lax.rem(number, slots) < count_ref[number // slots]
            beyond = jnp.where(live, 0, total)
            key_slot = key_slot + jnp.where(lane // BLOCK == piece, beyond, 0)
        key_slot_ref[pl.ds(index, 1), :] = key_slot

    repeat(0, tiles, fill)
    for slot in range(slots):
        gates_ref[pl.ds(slot, 1), :] = gate_ref[pl.ds(chosen_ref[me, slot], 1), :]
    for slot in range(slots):
        rows_copy(slot).wait()


def local(
    tokens, norm_gain, w_query, w_key, w_value, w_out, router_gate, chosen_blocks, block_counts
):
    seq_count = lax.axis_size("seq")
    section_count = lax.axis_size("section")
    me = lax.axis_index("seq")
    tok_rows, width = tokens.shape
    slots = chosen_blocks.shape[1]
    capacity = slots * BLOCK
    depth = section_count * width
    query_cols = w_query.shape[1]
    kv_cols = w_key.shape[1]
    ratio = HEADS // KV_HEADS
    line = seq_count // 2

    vmem = pl.BlockSpec(memory_space=pltpu.VMEM)
    smem = pl.BlockSpec(memory_space=pltpu.SMEM)
    anywhere = pl.BlockSpec(memory_space=pl.ANY)
    bf16 = jnp.bfloat16
    dma = pltpu.SemaphoreType.DMA
    tile = math.gcd(seq_count * capacity, 512)
    picked, gates, key_slot = pl.pallas_call(
        functools.partial(pick, seq_count),
        out_shape=(
            jax.ShapeDtypeStruct((capacity, width), tokens.dtype),
            jax.ShapeDtypeStruct((slots, BLOCK), jnp.float32),
            jax.ShapeDtypeStruct((seq_count * capacity // tile, tile), jnp.int32),
        ),
        in_specs=[anywhere, vmem, smem, smem],
        out_specs=(vmem, vmem, vmem),
        scratch_shapes=[dma((slots,))],
    )(tokens, router_gate.reshape(tok_rows // BLOCK, BLOCK), chosen_blocks, block_counts)
    new_rows = pl.pallas_call(
        functools.partial(kernel, seq_count, section_count),
        out_shape=jax.ShapeDtypeStruct((capacity, width), tokens.dtype),
        in_specs=[vmem] * 4 + [anywhere] * 4,
        out_specs=vmem,
        scratch_shapes=[
            pltpu.VMEM((section_count, 2, capacity, width), bf16),
            pltpu.VMEM((2, slots, BLOCK), jnp.float32),
            pltpu.VMEM((2 * capacity, depth), bf16),
            pltpu.VMEM((depth, kv_cols), bf16),
            pltpu.VMEM((depth, kv_cols), bf16),
            pltpu.VMEM((2, depth, query_cols // 2), bf16),
            pltpu.VMEM((2, w_out.shape[0] * seq_count, w_out.shape[1] // 2), bf16),
            pltpu.VMEM((seq_count * capacity, 2 * kv_cols), bf16),
            pltpu.VMEM((2, query_cols // HEAD_DIM, capacity, HEAD_DIM), bf16),
            pltpu.VMEM((ratio * capacity, HEAD_DIM), jnp.float32),
            pltpu.VMEM((ratio * capacity, 1), jnp.float32),
            pltpu.VMEM((section_count, 2, capacity, query_cols), bf16),
            pltpu.VMEM((2, capacity, width // 2), bf16),
            pltpu.VMEM((2, capacity, width // 2), bf16),
            dma((7, seq_count)),
            dma((2, 7, line)),
            dma((7, line)),
            dma((6,)),
            dma((2, section_count)),
            dma((2, section_count)),
            dma((2, section_count)),
            dma((2, section_count)),
            dma((2,)),
            dma((2,)),
            dma((2,)),
            dma((2,)),
        ],
        compiler_params=pltpu.CompilerParams(collective_id=0, has_side_effects=True),
    )(
        picked,
        norm_gain[None, :],
        gates,
        key_slot,
        w_query,
        w_key,
        w_value,
        w_out,
    )
    mixed = tokens.reshape(tok_rows // BLOCK, BLOCK, width)
    number = lax.broadcasted_iota(jnp.int32, (tok_rows // BLOCK, 1, 1), 0)
    for slot in range(slots):
        hit = (number == chosen_blocks[me, slot]) & (slot < block_counts[me])
        mixed = jnp.where(hit, new_rows[None, slot * BLOCK : (slot + 1) * BLOCK], mixed)
    return mixed.reshape(tok_rows, width)


def solution(mesh):
    return jax.shard_map(
        local,
        mesh=mesh,
        in_specs=(
            P("seq", "section"),
            P(),
            P("seq", "section"),
            P("seq", "section"),
            P("seq", "section"),
            P("seq", "section"),
            P("seq"),
            P(),
            P(),
        ),
        out_specs=P("seq", "section"),
        check_vma=False,
    )
```

```python
import functools
import math

import jax
import jax.numpy as jnp
from jax import lax
from jax.experimental import pallas as pl
from jax.experimental.pallas import tpu as pltpu
from jax.sharding import PartitionSpec as P

HEADS = 16
KV_HEADS = 4
HEAD_DIM = 128
BLOCK = 128
EPSILON = 1e-05
MESH = pl.DeviceIdType.MESH

KEY, VALUE, QUERY_A, QUERY_B, OUT_A, OUT_B, PANEL, GUEST_PANEL = range(8)


def repeat(low, high, body):
    if high - low <= 4:
        for step in range(low, high):
            body(step)
    elif high > low:

        def wrapped(step, carry):
            body(step)
            return carry

        lax.fori_loop(low, high, wrapped, 0)


def kernel(
    seq_count,
    section_count,
    tokens_ref,
    gain_ref,
    gate_ref,
    chosen_ref,
    count_ref,
    wq_in,
    wk_in,
    wv_in,
    wo_in,
    out_ref,
    rows_all,
    gate_rows,
    normed_ref,
    wk,
    wv,
    wq,
    wo,
    panel,
    queries_ref,
    numer_ref,
    denom_ref,
    heads_all,
    results,
    returned,
    recv,
    send_line,
    send_pair,
    own_sem,
    rows_send,
    rows_recv,
    heads_send,
    heads_recv,
    guest_send,
    guest_recv,
    back_send,
    back_recv,
    key_slots,
):
    me = lax.axis_index("seq")
    section = lax.axis_index("section")
    line = seq_count // 2
    spot = me // 2
    core = lax.rem(me, 2)
    pair = spot * 2 + 1 - core
    slots = chosen_ref.shape[0] // seq_count
    capacity, width = out_ref.shape
    kv_cols = wk_in.shape[1]
    groups = kv_cols // HEAD_DIM
    ratio = HEADS // KV_HEADS
    half_q = wq_in.shape[1] // 2
    half_o = wo_in.shape[1] // 2
    depth = section_count * width
    first, last = 1, line - 2
    active = (spot >= first) & (spot <= last)
    has_guest = (spot == first) | (spot == last)
    near = jnp.where(spot * 2 < line, 1, -1)
    guest_spot = spot - near
    guest = me - 2 * near
    host = me + 2 * near

    def rows_of(block, size):
        return pl.ds(pl.multiple_of(block * size, size), size)

    def full(chunk, block):
        if chunk == KEY:
            return wk.at[rows_of(block, wk_in.shape[0]), :]
        if chunk == VALUE:
            return wv.at[rows_of(block, wv_in.shape[0]), :]
        if chunk in (QUERY_A, QUERY_B):
            return wq.at[chunk - QUERY_A, rows_of(block, wq_in.shape[0]), :]
        if chunk in (PANEL, GUEST_PANEL):
            return panel.at[rows_of(block, capacity), :]
        return wo.at[chunk - OUT_A, rows_of(block, wo_in.shape[0]), :]

    def own(chunk):
        if chunk == KEY:
            return wk_in
        if chunk == VALUE:
            return wv_in
        if chunk in (QUERY_A, QUERY_B):
            return wq_in.at[:, pl.ds((chunk - QUERY_A) * half_q, half_q)]
        return wo_in.at[:, pl.ds((chunk - OUT_A) * half_o, half_o)]

    def transfer(chunk, block, send_sem, target, mine):
        return pltpu.make_async_remote_copy(
            src_ref=own(chunk) if mine else full(chunk, block),
            dst_ref=full(chunk, block),
            send_sem=send_sem,
            recv_sem=recv.at[min(chunk, PANEL), block],
            device_id={"seq": target},
            device_id_type=MESH,
        )

    def along(chunk, source, sign, mine):
        way = (1 - sign) // 2
        return transfer(
            chunk, source * 2 + core, send_line.at[way, min(chunk, PANEL), source], me + 2 * sign, mine
        )

    def across(chunk, source, mine):
        return transfer(
            chunk, source * 2 + core, send_pair.at[min(chunk, PANEL), source], pair, mine
        )

    def onward(sign):
        return (spot + sign >= first) & (spot + sign <= last)

    def begin(chunk, source):
        mine = chunk < PANEL
        for sign in (1, -1):

            @pl.when(onward(sign))
            def _():
                along(chunk, source, sign, mine).start()

        @pl.when(active)
        def _():
            across(chunk, source, mine).start()

    def relay(chunk, step, sign):
        source = spot - sign * step
        low, high = (first, last) if chunk >= PANEL else (0, line - 1)
        valid = active & (source >= low) & (source <= high)
        if chunk == GUEST_PANEL:
            valid = active & (source == jnp.where(sign > 0, first, last))
            source = source - sign

        @pl.when(valid)
        def _():
            across(chunk, source, False).wait_recv()

            @pl.when(onward(sign))
            def _():
                along(chunk, source, sign, False).start()

            across(chunk, source, False).start()

    def relay_all(chunks, low, high, sides=(1, -1)):
        def body(step):
            for side in sides:
                for chunk in chunks:
                    relay(chunk, step, side * near)

        repeat(low, high, body)

    def await_pair(chunk):
        def body(source):
            transfer(
                chunk, source * 2 + 1 - core, send_pair.at[chunk, source], pair, False
            ).wait_recv()

        repeat(0, line, body)

    def finish_sends(chunk):
        def body(source):
            for sign in (1, -1):
                origin = jnp.clip(source, first, last) if chunk == PANEL else source

                @pl.when(onward(sign) & (origin * sign <= spot * sign))
                def _():
                    along(chunk, source, sign, False).wait_send()

            @pl.when(active)
            def _():
                across(chunk, source, False).wait_send()

        if chunk == PANEL:

            def guarded(source):
                pl.when(active)(lambda: body(source))

            repeat(0, line, guarded)
        else:
            repeat(0, line, body)

    def own_copy(chunk):
        return pltpu.make_async_copy(own(chunk), full(chunk, me), own_sem.at[chunk])

    def spread(buffer, send, receive, who, offset):
        peer = lax.rem(section + offset, section_count)
        return pltpu.make_async_remote_copy(
            src_ref=buffer.at[section, who],
            dst_ref=buffer.at[section, who],
            send_sem=send.at[who, offset],
            recv_sem=receive.at[who, section],
            device_id={"section": peer},
            device_id_type=MESH,
        )

    def await_spread(buffer, send, receive, who):
        for offset in range(1, section_count):
            peer = lax.rem(section + offset, section_count)
            pltpu.make_async_remote_copy(
                src_ref=buffer.at[peer, who],
                dst_ref=buffer.at[peer, who],
                send_sem=send.at[who, offset],
                recv_sem=receive.at[who, peer],
                device_id={"section": peer},
                device_id_type=MESH,
            ).wait_recv()

    def to_host():
        return (
            pltpu.make_async_remote_copy(
                src_ref=rows_all.at[section, 0],
                dst_ref=rows_all.at[section, 1],
                send_sem=guest_send.at[0],
                recv_sem=guest_recv.at[0],
                device_id={"seq": host},
                device_id_type=MESH,
            ),
            pltpu.make_async_remote_copy(
                src_ref=gate_rows.at[0],
                dst_ref=gate_rows.at[1],
                send_sem=guest_send.at[1],
                recv_sem=guest_recv.at[1],
                device_id={"seq": host},
                device_id_type=MESH,
            ),
        )

    def give_back(half, target):
        return pltpu.make_async_remote_copy(
            src_ref=results.at[half],
            dst_ref=returned.at[half],
            send_sem=back_send.at[half],
            recv_sem=back_recv.at[half],
            device_id={"seq": target},
            device_id_type=MESH,
        )

    for slot in range(slots):
        number = chosen_ref[me * slots + slot]
        rows = tokens_ref[:BLOCK, :]
        gates = gate_ref[:1, :]
        for block in range(1, gate_ref.shape[0]):
            rows = jnp.where(
                jnp.full(rows.shape, number, jnp.int32) == block,
                tokens_ref[block * BLOCK : (block + 1) * BLOCK, :],
                rows,
            )
            gates = jnp.where(
                jnp.full(gates.shape, number, jnp.int32) == block,
                gate_ref[block : block + 1, :],
                gates,
            )
        rows_all[section, 0, pl.ds(slot * BLOCK, BLOCK), :] = rows
        gate_rows[0, pl.ds(slot, 1), :] = gates
    total = seq_count * capacity
    tiles, tile = key_slots.shape
    lane = lax.broadcasted_iota(jnp.int32, (1, tile), 1)

    def fill(index):
        key_slot = lane + index * tile
        for piece in range(tile // BLOCK):
            place = index * (tile // BLOCK) + piece
            within = lax.rem(place, slots)
            count = jnp.full((1, tile), count_ref[place // slots], jnp.int32)
            key_slot = jnp.where(
                (lane // BLOCK == piece) & (count <= within), total, key_slot
            )
        key_slots[pl.ds(index, 1), :] = key_slot

    repeat(0, tiles, fill)

    barrier = pltpu.get_barrier_semaphore()

    @pl.when(spot + 1 < line)
    def _():
        pl.semaphore_signal(barrier, inc=1, device_id={"seq": me + 2}, device_id_type=MESH)

    @pl.when(spot > 0)
    def _():
        pl.semaphore_signal(barrier, inc=1, device_id={"seq": me - 2}, device_id_type=MESH)

    pl.semaphore_signal(barrier, inc=1, device_id={"seq": pair}, device_id_type=MESH)
    for offset in range(1, section_count):
        peer = lax.rem(section + offset, section_count)
        pl.semaphore_signal(barrier, inc=1, device_id={"section": peer}, device_id_type=MESH)
    neighbours = jnp.where(spot + 1 < line, 1, 0) + jnp.where(spot > 0, 1, 0)
    pl.semaphore_wait(barrier, section_count + neighbours)

    weights_chunks = (KEY, VALUE, QUERY_A, QUERY_B, OUT_A, OUT_B)

    @pl.when(jnp.logical_not(active))
    def _():
        for copy in to_host():
            copy.start()
        for chunk in weights_chunks:
            begin(chunk, spot)

    def gate_column(who):
        wide = gate_rows[who]
        square = lax.broadcasted_iota(jnp.int32, (BLOCK, BLOCK), 0) == lax.broadcasted_iota(
            jnp.int32, (BLOCK, BLOCK), 1
        )
        return jnp.concatenate(
            [
                jnp.sum(jnp.where(square, wide[slot : slot + 1, :], 0.0), axis=1, keepdims=True)
                for slot in range(slots)
            ],
            axis=0,
        )

    def normalise(who):
        square_sum = jnp.zeros((capacity, 1), jnp.float32)
        for part in range(section_count):
            features = rows_all[part, who].astype(jnp.float32)
            square_sum += jnp.sum(features * features, axis=-1, keepdims=True)
        factor = lax.rsqrt(square_sum / depth + EPSILON)
        for part in range(section_count):
            cols = pl.ds(part * width, width)
            normed_ref[pl.ds(who * capacity, capacity), cols] = (
                rows_all[part, who].astype(jnp.float32) * factor * gain_ref[:, cols]
            ).astype(jnp.bfloat16)

    def attend(who, owner):
        scale = HEAD_DIM ** (-0.5)
        tall = lax.broadcasted_iota(jnp.int32, (ratio * capacity, 1), 0)
        query_slot = lax.rem(tall, capacity) + owner * capacity
        for group in range(groups):
            numer_ref[...] = jnp.zeros_like(numer_ref)
            denom_ref[...] = jnp.zeros_like(denom_ref)

            def fold(index):
                start = index * tile
                key_slot = key_slots[pl.ds(index, 1), :]
                rows = pl.ds(pl.multiple_of(start, tile), tile)
                keys = panel[rows, pl.ds(group * HEAD_DIM, HEAD_DIM)]
                values = panel[rows, pl.ds(kv_cols + group * HEAD_DIM, HEAD_DIM)]
                wide = queries_ref[who, pl.ds(group * ratio, ratio)].reshape(
                    ratio * capacity, HEAD_DIM
                )
                scores = (
                    lax.dot_general(
                        wide, keys, (((1,), (1,)), ((), ())), preferred_element_type=jnp.float32
                    )
                    * scale
                )
                weights = jnp.where(key_slot <= query_slot, jnp.exp(scores), 0.0)
                denom_ref[...] += jnp.sum(weights, axis=-1, keepdims=True)
                numer_ref[...] += jnp.dot(
                    weights.astype(jnp.bfloat16), values, preferred_element_type=jnp.float32
                )

            repeat(0, total // tile, fold)
            safe = jnp.where(denom_ref[...] > 0, denom_ref[...], 1.0)
            result = (numer_ref[...] / safe).astype(jnp.bfloat16)
            for head in range(ratio):
                cols = pl.ds((group * ratio + head) * HEAD_DIM, HEAD_DIM)
                heads_all[section, who, :, cols] = result[head * capacity : (head + 1) * capacity]

    def finish(who, half):
        update = jnp.zeros((capacity, half_o), jnp.float32)
        head_cols = heads_all.shape[3]
        for part in range(section_count):
            update += jnp.dot(
                heads_all[part, who],
                wo[half, pl.ds(part * head_cols, head_cols), :],
                preferred_element_type=jnp.float32,
            )
        cols = pl.ds(half * half_o, half_o)
        return (
            rows_all[section, who, :, cols].astype(jnp.float32) + gate_column(who) * update
        ).astype(out_ref.dtype)

    @pl.when(active)
    def _():
        begin(KEY, spot)
        begin(VALUE, spot)
        for offset in range(1, section_count):
            spread(rows_all, rows_send, rows_recv, 0, offset).start()

        @pl.when(has_guest)
        def _():
            for copy in to_host():
                copy.wait_recv()
            for offset in range(1, section_count):
                spread(rows_all, rows_send, rows_recv, 1, offset).start()

        for chunk in weights_chunks:
            own_copy(chunk).start()
        relay_all((KEY, VALUE), 1, 2, (1,))
        begin(QUERY_A, spot)
        begin(QUERY_B, spot)
        relay_all((KEY, VALUE), 1, 2, (-1,))
        relay_all((KEY, VALUE), 2, line)
        await_spread(rows_all, rows_send, rows_recv, 0)
        normalise(0)
        relay_all((QUERY_A, QUERY_B), 1, 2, (1,))

        @pl.when(has_guest)
        def _():
            await_spread(rows_all, rows_send, rows_recv, 1)
            normalise(1)

        for chunk in (KEY, VALUE):
            await_pair(chunk)
            own_copy(chunk).wait()
        for position, weight in enumerate((wk, wv)):
            sums = jnp.dot(
                normed_ref[...], weight[...], preferred_element_type=jnp.float32
            ).astype(jnp.bfloat16)
            cols = pl.ds(position * kv_cols, kv_cols)
            panel[rows_of(me, capacity), cols] = sums[:capacity]

            @pl.when(has_guest)
            def _():
                panel[rows_of(guest, capacity), cols] = sums[capacity:]

        begin(PANEL, spot)

        @pl.when(has_guest)
        def _():
            begin(GUEST_PANEL, guest_spot)

        begin(OUT_A, spot)
        begin(OUT_B, spot)
        relay_all((QUERY_A, QUERY_B), 1, 2, (-1,))
        relay_all((QUERY_A, QUERY_B), 2, line)
        relay_all((PANEL, GUEST_PANEL), 1, line)
        relay_all((OUT_A, OUT_B), 1, 2, (1,))
        heads_half = half_q // HEAD_DIM
        for half in range(2):
            await_pair(QUERY_A + half)
            own_copy(QUERY_A + half).wait()
            sums = jnp.dot(
                normed_ref[...], wq[half], preferred_element_type=jnp.float32
            ).astype(jnp.bfloat16)
            for who in range(2):
                for head in range(heads_half):
                    queries_ref[who, half * heads_half + head] = sums[
                        who * capacity : (who + 1) * capacity,
                        head * HEAD_DIM : (head + 1) * HEAD_DIM,
                    ]
        await_pair(PANEL)

        @pl.when(has_guest)
        def _():
            attend(1, guest)
            for offset in range(1, section_count):
                spread(heads_all, heads_send, heads_recv, 1, offset).start()

        attend(0, me)
        for offset in range(1, section_count):
            spread(heads_all, heads_send, heads_recv, 0, offset).start()
        relay_all((OUT_A, OUT_B), 1, 2, (-1,))
        relay_all((OUT_A, OUT_B), 2, line)
        for half in range(2):
            await_pair(OUT_A + half)
            own_copy(OUT_A + half).wait()

        @pl.when(has_guest)
        def _():
            await_spread(heads_all, heads_send, heads_recv, 1)
            for half in range(2):
                results[half] = finish(1, half)
                give_back(half, guest).start()

        await_spread(heads_all, heads_send, heads_recv, 0)
        for half in range(2):
            out_ref[:, pl.ds(half * half_o, half_o)] = finish(0, half)
        for offset in range(1, section_count):
            spread(rows_all, rows_send, rows_recv, 0, offset).wait_send()
            spread(heads_all, heads_send, heads_recv, 0, offset).wait_send()

        @pl.when(has_guest)
        def _():
            for offset in range(1, section_count):
                spread(rows_all, rows_send, rows_recv, 1, offset).wait_send()
                spread(heads_all, heads_send, heads_recv, 1, offset).wait_send()
            for half in range(2):
                give_back(half, guest).wait_send()

    for chunk in weights_chunks + (PANEL,):
        finish_sends(chunk)

    @pl.when(jnp.logical_not(active))
    def _():
        for copy in to_host():
            copy.wait_send()
        for half in range(2):
            give_back(half, host).wait_recv()
            out_ref[:, pl.ds(half * half_o, half_o)] = returned[half]


def put(tokens_ref, rows_ref, chosen_ref, count_ref, mixed_ref):
    me = lax.axis_index("seq")
    mixed_ref[...] = tokens_ref[...]
    slots = rows_ref.shape[0] // BLOCK
    for slot in range(slots):

        @pl.when(slot < count_ref[me])
        def _():
            start = pl.multiple_of(chosen_ref[me * slots + slot] * BLOCK, BLOCK)
            mixed_ref[pl.ds(start, BLOCK), :] = rows_ref[slot * BLOCK : (slot + 1) * BLOCK, :]


def local(
    tokens, norm_gain, w_query, w_key, w_value, w_out, router_gate, chosen_blocks, block_counts
):
    seq_count = lax.axis_size("seq")
    section_count = lax.axis_size("section")
    tok_rows, width = tokens.shape
    slots = chosen_blocks.shape[1]
    capacity = slots * BLOCK
    depth = section_count * width
    query_cols = w_query.shape[1]
    kv_cols = w_key.shape[1]
    ratio = HEADS // KV_HEADS
    line = seq_count // 2

    vmem = pl.BlockSpec(memory_space=pltpu.VMEM)
    smem = pl.BlockSpec(memory_space=pltpu.SMEM)
    anywhere = pl.BlockSpec(memory_space=pl.ANY)
    bf16 = jnp.bfloat16
    dma = pltpu.SemaphoreType.DMA
    tile = math.gcd(seq_count * capacity, 512)
    blocks = chosen_blocks.reshape(-1)
    new_rows = pl.pallas_call(
        functools.partial(kernel, seq_count, section_count),
        out_shape=jax.ShapeDtypeStruct((capacity, width), tokens.dtype),
        in_specs=[vmem] * 3 + [smem] * 2 + [anywhere] * 4,
        out_specs=vmem,
        scratch_shapes=[
            pltpu.VMEM((section_count, 2, capacity, width), bf16),
            pltpu.VMEM((2, slots, BLOCK), jnp.float32),
            pltpu.VMEM((2 * capacity, depth), bf16),
            pltpu.VMEM((depth, kv_cols), bf16),
            pltpu.VMEM((depth, kv_cols), bf16),
            pltpu.VMEM((2, depth, query_cols // 2), bf16),
            pltpu.VMEM((2, w_out.shape[0] * seq_count, w_out.shape[1] // 2), bf16),
            pltpu.VMEM((seq_count * capacity, 2 * kv_cols), bf16),
            pltpu.VMEM((2, query_cols // HEAD_DIM, capacity, HEAD_DIM), bf16),
            pltpu.VMEM((ratio * capacity, HEAD_DIM), jnp.float32),
            pltpu.VMEM((ratio * capacity, 1), jnp.float32),
            pltpu.VMEM((section_count, 2, capacity, query_cols), bf16),
            pltpu.VMEM((2, capacity, width // 2), bf16),
            pltpu.VMEM((2, capacity, width // 2), bf16),
            dma((7, seq_count)),
            dma((2, 7, line)),
            dma((7, line)),
            dma((6,)),
            dma((2, section_count)),
            dma((2, section_count)),
            dma((2, section_count)),
            dma((2, section_count)),
            dma((2,)),
            dma((2,)),
            dma((2,)),
            dma((2,)),
            pltpu.VMEM((seq_count * capacity // tile, tile), jnp.int32),
        ],
        compiler_params=pltpu.CompilerParams(collective_id=0, has_side_effects=True),
    )(
        tokens,
        norm_gain[None, :],
        router_gate.reshape(tok_rows // BLOCK, BLOCK),
        blocks,
        block_counts,
        w_query,
        w_key,
        w_value,
        w_out,
    )
    return pl.pallas_call(
        put,
        out_shape=jax.ShapeDtypeStruct(tokens.shape, tokens.dtype),
        in_specs=[vmem, vmem, smem, smem],
        out_specs=vmem,
    )(tokens, new_rows, blocks, block_counts)


def solution(mesh):
    return jax.shard_map(
        local,
        mesh=mesh,
        in_specs=(
            P("seq", "section"),
            P(),
            P("seq", "section"),
            P("seq", "section"),
            P("seq", "section"),
            P("seq", "section"),
            P("seq"),
            P(),
            P(),
        ),
        out_specs=P("seq", "section"),
        check_vma=False,
    )
```

```python
import functools
import math

import jax
import jax.numpy as jnp
from jax import lax
from jax.experimental import pallas as pl
from jax.experimental.pallas import tpu as pltpu
from jax.sharding import PartitionSpec as P

HEADS = 16
KV_HEADS = 4
HEAD_DIM = 128
BLOCK = 128
EPSILON = 1e-05
MESH = pl.DeviceIdType.MESH

KEY, VALUE, QUERY_A, QUERY_B, OUT_A, OUT_B, PANEL, GUEST_PANEL = range(8)


def repeat(low, high, body):
    if high - low <= 4:
        for step in range(low, high):
            body(step)
    elif high > low:

        def wrapped(step, carry):
            body(step)
            return carry

        lax.fori_loop(low, high, wrapped, 0)


def kernel(
    seq_count,
    section_count,
    tokens_ref,
    gain_ref,
    gate_ref,
    chosen_ref,
    count_ref,
    wq_in,
    wk_in,
    wv_in,
    wo_in,
    out_ref,
    rows_all,
    gate_rows,
    normed_ref,
    wk,
    wv,
    wq,
    wo,
    panel,
    queries_ref,
    numer_ref,
    denom_ref,
    heads_all,
    results,
    returned,
    recv,
    send_line,
    send_pair,
    own_sem,
    rows_send,
    rows_recv,
    heads_send,
    heads_recv,
    guest_send,
    guest_recv,
    back_send,
    back_recv,
    key_slots,
):
    me = lax.axis_index("seq")
    section = lax.axis_index("section")
    line = seq_count // 2
    spot = me // 2
    core = lax.rem(me, 2)
    pair = spot * 2 + 1 - core
    slots = chosen_ref.shape[0] // seq_count
    capacity, width = out_ref.shape
    kv_cols = wk_in.shape[1]
    groups = kv_cols // HEAD_DIM
    ratio = HEADS // KV_HEADS
    half_q = wq_in.shape[1] // 2
    half_o = wo_in.shape[1] // 2
    depth = section_count * width
    first, last = 1, line - 2
    active = (spot >= first) & (spot <= last)
    has_guest = (spot == first) | (spot == last)
    near = jnp.where(spot * 2 < line, 1, -1)
    guest_spot = spot - near
    guest = me - 2 * near
    host = me + 2 * near

    square = section_count == 4
    offsets = (1, 2) if square else tuple(range(1, section_count))

    def rows_of(block, size):
        return pl.ds(pl.multiple_of(block * size, size), size)

    def full(chunk, block):
        if chunk == KEY:
            return wk.at[rows_of(block, wk_in.shape[0]), :]
        if chunk == VALUE:
            return wv.at[rows_of(block, wv_in.shape[0]), :]
        if chunk in (QUERY_A, QUERY_B):
            return wq.at[chunk - QUERY_A, rows_of(block, wq_in.shape[0]), :]
        if chunk in (PANEL, GUEST_PANEL):
            return panel.at[rows_of(block, capacity), :]
        return wo.at[chunk - OUT_A, rows_of(block, wo_in.shape[0]), :]

    def own(chunk):
        if chunk == KEY:
            return wk_in
        if chunk == VALUE:
            return wv_in
        if chunk in (QUERY_A, QUERY_B):
            return wq_in.at[:, pl.ds((chunk - QUERY_A) * half_q, half_q)]
        return wo_in.at[:, pl.ds((chunk - OUT_A) * half_o, half_o)]

    def transfer(chunk, block, send_sem, target, mine):
        return pltpu.make_async_remote_copy(
            src_ref=own(chunk) if mine else full(chunk, block),
            dst_ref=full(chunk, block),
            send_sem=send_sem,
            recv_sem=recv.at[min(chunk, PANEL), block],
            device_id={"seq": target},
            device_id_type=MESH,
        )

    def along(chunk, source, sign, mine):
        way = (1 - sign) // 2
        return transfer(
            chunk, source * 2 + core, send_line.at[way, min(chunk, PANEL), source], me + 2 * sign, mine
        )

    def across(chunk, source, mine):
        return transfer(
            chunk, source * 2 + core, send_pair.at[min(chunk, PANEL), source], pair, mine
        )

    def onward(sign):
        return (spot + sign >= first) & (spot + sign <= last)

    def begin(chunk, source):
        mine = chunk < PANEL
        for sign in (1, -1):

            @pl.when(onward(sign))
            def _():
                along(chunk, source, sign, mine).start()

        @pl.when(active)
        def _():
            across(chunk, source, mine).start()

    def relay(chunk, step, sign):
        source = spot - sign * step
        low, high = (first, last) if chunk >= PANEL else (0, line - 1)
        valid = active & (source >= low) & (source <= high)
        if chunk == GUEST_PANEL:
            valid = active & (source == jnp.where(sign > 0, first, last))
            source = source - sign

        @pl.when(valid)
        def _():
            across(chunk, source, False).wait_recv()

            @pl.when(onward(sign))
            def _():
                along(chunk, source, sign, False).start()

            across(chunk, source, False).start()

    def relay_all(chunks, low, high, sides=(1, -1)):
        def body(step):
            for side in sides:
                for chunk in chunks:
                    relay(chunk, step, side * near)

        repeat(low, high, body)

    def await_pair(chunk):
        def body(source):
            transfer(
                chunk, source * 2 + 1 - core, send_pair.at[chunk, source], pair, False
            ).wait_recv()

        repeat(0, line, body)

    def finish_sends(chunk):
        def body(source):
            for sign in (1, -1):
                origin = jnp.clip(source, first, last) if chunk == PANEL else source

                @pl.when(onward(sign) & (origin * sign <= spot * sign))
                def _():
                    along(chunk, source, sign, False).wait_send()

            @pl.when(active)
            def _():
                across(chunk, source, False).wait_send()

        if chunk == PANEL:

            def guarded(source):
                pl.when(active)(lambda: body(source))

            repeat(0, line, guarded)
        else:
            repeat(0, line, body)

    def own_copy(chunk):
        return pltpu.make_async_copy(own(chunk), full(chunk, me), own_sem.at[chunk])

    def beside(offset):
        if not square:
            return lax.rem(section + offset, section_count)
        if offset == 1:
            return section + 1 - 2 * lax.rem(section, 2)
        return section + 2 - 4 * (section // 2)

    def spread(buffer, send, receive, who, offset):
        return pltpu.make_async_remote_copy(
            src_ref=buffer.at[section, who],
            dst_ref=buffer.at[section, who],
            send_sem=send.at[who, offset],
            recv_sem=receive.at[who, section],
            device_id={"section": beside(offset)},
            device_id_type=MESH,
        )

    def await_direct(buffer, send, receive, who, offset):
        peer = beside(offset)
        pltpu.make_async_remote_copy(
            src_ref=buffer.at[peer, who],
            dst_ref=buffer.at[peer, who],
            send_sem=send.at[who, offset],
            recv_sem=receive.at[who, peer],
            device_id={"section": peer},
            device_id_type=MESH,
        ).wait_recv()

    def passed_on(buffer, send, receive, who, half, block, target, mark):
        part = buffer.at[block, who, pl.ds(half * (capacity // 2), capacity // 2), :]
        return pltpu.make_async_remote_copy(
            src_ref=part,
            dst_ref=part,
            send_sem=send.at[who, 3 * half],
            recv_sem=receive.at[who, mark],
            device_id={"section": target},
            device_id_type=MESH,
        )

    def outgoing(buffer, send, receive, who, half):
        block, target = beside(1 + half), beside(2 - half)
        mark = target if half else block
        return passed_on(buffer, send, receive, who, half, block, target, mark)

    def pass_on(buffer, send, receive, who):
        if square:
            for half in range(2):
                await_direct(buffer, send, receive, who, 1 + half)
                outgoing(buffer, send, receive, who, half).start()

    def await_spread(buffer, send, receive, who):
        if square:
            block = 3 - section
            for half in range(2):
                mark = section if half else block
                passed_on(
                    buffer, send, receive, who, half, block, beside(1), mark
                ).wait_recv()
        else:
            for offset in offsets:
                await_direct(buffer, send, receive, who, offset)

    def finish_spread(buffer, send, receive, who):
        for offset in offsets:
            spread(buffer, send, receive, who, offset).wait_send()
        if square:
            for half in range(2):
                outgoing(buffer, send, receive, who, half).wait_send()

    def to_host():
        return (
            pltpu.make_async_remote_copy(
                src_ref=rows_all.at[section, 0],
                dst_ref=rows_all.at[section, 1],
                send_sem=guest_send.at[0],
                recv_sem=guest_recv.at[0],
                device_id={"seq": host},
                device_id_type=MESH,
            ),
            pltpu.make_async_remote_copy(
                src_ref=gate_rows.at[0],
                dst_ref=gate_rows.at[1],
                send_sem=guest_send.at[1],
                recv_sem=guest_recv.at[1],
                device_id={"seq": host},
                device_id_type=MESH,
            ),
        )

    def give_back(half, target):
        return pltpu.make_async_remote_copy(
            src_ref=results.at[half],
            dst_ref=returned.at[half],
            send_sem=back_send.at[half],
            recv_sem=back_recv.at[half],
            device_id={"seq": target},
            device_id_type=MESH,
        )

    for slot in range(slots):
        number = chosen_ref[me * slots + slot]
        rows = tokens_ref[:BLOCK, :]
        gates = gate_ref[:1, :]
        for block in range(1, gate_ref.shape[0]):
            rows = jnp.where(
                jnp.full(rows.shape, number, jnp.int32) == block,
                tokens_ref[block * BLOCK : (block + 1) * BLOCK, :],
                rows,
            )
            gates = jnp.where(
                jnp.full(gates.shape, number, jnp.int32) == block,
                gate_ref[block : block + 1, :],
                gates,
            )
        rows_all[section, 0, pl.ds(slot * BLOCK, BLOCK), :] = rows
        gate_rows[0, pl.ds(slot, 1), :] = gates
    total = seq_count * capacity
    tiles, tile = key_slots.shape
    lane = lax.broadcasted_iota(jnp.int32, (1, tile), 1)

    def fill(index):
        key_slot = lane + index * tile
        for piece in range(tile // BLOCK):
            place = index * (tile // BLOCK) + piece
            within = lax.rem(place, slots)
            count = jnp.full((1, tile), count_ref[place // slots], jnp.int32)
            key_slot = jnp.where(
                (lane // BLOCK == piece) & (count <= within), total, key_slot
            )
        key_slots[pl.ds(index, 1), :] = key_slot

    repeat(0, tiles, fill)

    barrier = pltpu.get_barrier_semaphore()

    @pl.when(spot + 1 < line)
    def _():
        pl.semaphore_signal(barrier, inc=1, device_id={"seq": me + 2}, device_id_type=MESH)

    @pl.when(spot > 0)
    def _():
        pl.semaphore_signal(barrier, inc=1, device_id={"seq": me - 2}, device_id_type=MESH)

    pl.semaphore_signal(barrier, inc=1, device_id={"seq": pair}, device_id_type=MESH)
    for offset in range(1, section_count):
        peer = lax.rem(section + offset, section_count)
        pl.semaphore_signal(barrier, inc=1, device_id={"section": peer}, device_id_type=MESH)
    neighbours = jnp.where(spot + 1 < line, 1, 0) + jnp.where(spot > 0, 1, 0)
    pl.semaphore_wait(barrier, section_count + neighbours)

    weights_chunks = (KEY, VALUE, QUERY_A, QUERY_B, OUT_A, OUT_B)

    @pl.when(jnp.logical_not(active))
    def _():
        for copy in to_host():
            copy.start()
        for chunk in weights_chunks:
            begin(chunk, spot)

    def gate_column(who):
        wide = gate_rows[who]
        square = lax.broadcasted_iota(jnp.int32, (BLOCK, BLOCK), 0) == lax.broadcasted_iota(
            jnp.int32, (BLOCK, BLOCK), 1
        )
        return jnp.concatenate(
            [
                jnp.sum(jnp.where(square, wide[slot : slot + 1, :], 0.0), axis=1, keepdims=True)
                for slot in range(slots)
            ],
            axis=0,
        )

    def normalise(who):
        square_sum = jnp.zeros((capacity, 1), jnp.float32)
        for part in range(section_count):
            features = rows_all[part, who].astype(jnp.float32)
            square_sum += jnp.sum(features * features, axis=-1, keepdims=True)
        factor = lax.rsqrt(square_sum / depth + EPSILON)
        for part in range(section_count):
            cols = pl.ds(part * width, width)
            normed_ref[pl.ds(who * capacity, capacity), cols] = (
                rows_all[part, who].astype(jnp.float32) * factor * gain_ref[:, cols]
            ).astype(jnp.bfloat16)

    def attend(who, owner):
        scale = HEAD_DIM ** (-0.5)
        tall = lax.broadcasted_iota(jnp.int32, (ratio * capacity, 1), 0)
        query_slot = lax.rem(tall, capacity) + owner * capacity
        for group in range(groups):
            numer_ref[...] = jnp.zeros_like(numer_ref)
            denom_ref[...] = jnp.zeros_like(denom_ref)

            def fold(index):
                start = index * tile
                key_slot = key_slots[pl.ds(index, 1), :]
                rows = pl.ds(pl.multiple_of(start, tile), tile)
                keys = panel[rows, pl.ds(group * HEAD_DIM, HEAD_DIM)]
                values = panel[rows, pl.ds(kv_cols + group * HEAD_DIM, HEAD_DIM)]
                wide = queries_ref[who, pl.ds(group * ratio, ratio)].reshape(
                    ratio * capacity, HEAD_DIM
                )
                scores = (
                    lax.dot_general(
                        wide, keys, (((1,), (1,)), ((), ())), preferred_element_type=jnp.float32
                    )
                    * scale
                )
                weights = jnp.where(key_slot <= query_slot, jnp.exp(scores), 0.0)
                denom_ref[...] += jnp.sum(weights, axis=-1, keepdims=True)
                numer_ref[...] += jnp.dot(
                    weights.astype(jnp.bfloat16), values, preferred_element_type=jnp.float32
                )

            repeat(0, total // tile, fold)
            safe = jnp.where(denom_ref[...] > 0, denom_ref[...], 1.0)
            result = (numer_ref[...] / safe).astype(jnp.bfloat16)
            for head in range(ratio):
                cols = pl.ds((group * ratio + head) * HEAD_DIM, HEAD_DIM)
                heads_all[section, who, :, cols] = result[head * capacity : (head + 1) * capacity]

    def finish(who, half):
        update = jnp.zeros((capacity, half_o), jnp.float32)
        head_cols = heads_all.shape[3]
        for part in range(section_count):
            update += jnp.dot(
                heads_all[part, who],
                wo[half, pl.ds(part * head_cols, head_cols), :],
                preferred_element_type=jnp.float32,
            )
        cols = pl.ds(half * half_o, half_o)
        return (
            rows_all[section, who, :, cols].astype(jnp.float32) + gate_column(who) * update
        ).astype(out_ref.dtype)

    @pl.when(active)
    def _():
        begin(KEY, spot)
        begin(VALUE, spot)
        for offset in offsets:
            spread(rows_all, rows_send, rows_recv, 0, offset).start()

        @pl.when(has_guest)
        def _():
            for copy in to_host():
                copy.wait_recv()
            for offset in offsets:
                spread(rows_all, rows_send, rows_recv, 1, offset).start()

        for chunk in weights_chunks:
            own_copy(chunk).start()
        relay_all((KEY, VALUE), 1, 2, (1,))
        begin(QUERY_A, spot)
        begin(QUERY_B, spot)
        pass_on(rows_all, rows_send, rows_recv, 0)
        relay_all((KEY, VALUE), 1, 2, (-1,))

        @pl.when(has_guest)
        def _():
            pass_on(rows_all, rows_send, rows_recv, 1)

        relay_all((KEY, VALUE), 2, line)
        await_spread(rows_all, rows_send, rows_recv, 0)
        normalise(0)
        relay_all((QUERY_A, QUERY_B), 1, 2, (1,))

        @pl.when(has_guest)
        def _():
            await_spread(rows_all, rows_send, rows_recv, 1)
            normalise(1)

        for chunk in (KEY, VALUE):
            await_pair(chunk)
            own_copy(chunk).wait()
        for position, weight in enumerate((wk, wv)):
            sums = jnp.dot(
                normed_ref[...], weight[...], preferred_element_type=jnp.float32
            ).astype(jnp.bfloat16)
            cols = pl.ds(position * kv_cols, kv_cols)
            panel[rows_of(me, capacity), cols] = sums[:capacity]

            @pl.when(has_guest)
            def _():
                panel[rows_of(guest, capacity), cols] = sums[capacity:]

        begin(PANEL, spot)

        @pl.when(has_guest)
        def _():
            begin(GUEST_PANEL, guest_spot)

        begin(OUT_A, spot)
        begin(OUT_B, spot)
        relay_all((QUERY_A, QUERY_B), 1, 2, (-1,))
        relay_all((QUERY_A, QUERY_B), 2, line)
        relay_all((PANEL, GUEST_PANEL), 1, line)
        relay_all((OUT_A, OUT_B), 1, 2, (1,))
        heads_half = half_q // HEAD_DIM
        for half in range(2):
            await_pair(QUERY_A + half)
            own_copy(QUERY_A + half).wait()
            sums = jnp.dot(
                normed_ref[...], wq[half], preferred_element_type=jnp.float32
            ).astype(jnp.bfloat16)
            for who in range(2):
                for head in range(heads_half):
                    queries_ref[who, half * heads_half + head] = sums[
                        who * capacity : (who + 1) * capacity,
                        head * HEAD_DIM : (head + 1) * HEAD_DIM,
                    ]
        await_pair(PANEL)

        @pl.when(has_guest)
        def _():
            attend(1, guest)
            for offset in offsets:
                spread(heads_all, heads_send, heads_recv, 1, offset).start()

        attend(0, me)
        for offset in offsets:
            spread(heads_all, heads_send, heads_recv, 0, offset).start()

        @pl.when(has_guest)
        def _():
            pass_on(heads_all, heads_send, heads_recv, 1)

        pass_on(heads_all, heads_send, heads_recv, 0)
        relay_all((OUT_A, OUT_B), 1, 2, (-1,))
        relay_all((OUT_A, OUT_B), 2, line)
        for half in range(2):
            await_pair(OUT_A + half)
            own_copy(OUT_A + half).wait()

        @pl.when(has_guest)
        def _():
            await_spread(heads_all, heads_send, heads_recv, 1)
            for half in range(2):
                results[half] = finish(1, half)
                give_back(half, guest).start()

        await_spread(heads_all, heads_send, heads_recv, 0)
        for half in range(2):
            out_ref[:, pl.ds(half * half_o, half_o)] = finish(0, half)
        finish_spread(rows_all, rows_send, rows_recv, 0)
        finish_spread(heads_all, heads_send, heads_recv, 0)

        @pl.when(has_guest)
        def _():
            finish_spread(rows_all, rows_send, rows_recv, 1)
            finish_spread(heads_all, heads_send, heads_recv, 1)
            for half in range(2):
                give_back(half, guest).wait_send()

    for chunk in weights_chunks + (PANEL,):
        finish_sends(chunk)

    @pl.when(jnp.logical_not(active))
    def _():
        for copy in to_host():
            copy.wait_send()
        for half in range(2):
            give_back(half, host).wait_recv()
            out_ref[:, pl.ds(half * half_o, half_o)] = returned[half]


def put(tokens_ref, rows_ref, chosen_ref, count_ref, mixed_ref):
    me = lax.axis_index("seq")
    mixed_ref[...] = tokens_ref[...]
    slots = rows_ref.shape[0] // BLOCK
    for slot in range(slots):

        @pl.when(slot < count_ref[me])
        def _():
            start = pl.multiple_of(chosen_ref[me * slots + slot] * BLOCK, BLOCK)
            mixed_ref[pl.ds(start, BLOCK), :] = rows_ref[slot * BLOCK : (slot + 1) * BLOCK, :]


def local(
    tokens, norm_gain, w_query, w_key, w_value, w_out, router_gate, chosen_blocks, block_counts
):
    seq_count = lax.axis_size("seq")
    section_count = lax.axis_size("section")
    tok_rows, width = tokens.shape
    slots = chosen_blocks.shape[1]
    capacity = slots * BLOCK
    depth = section_count * width
    query_cols = w_query.shape[1]
    kv_cols = w_key.shape[1]
    ratio = HEADS // KV_HEADS
    line = seq_count // 2

    vmem = pl.BlockSpec(memory_space=pltpu.VMEM)
    smem = pl.BlockSpec(memory_space=pltpu.SMEM)
    anywhere = pl.BlockSpec(memory_space=pl.ANY)
    bf16 = jnp.bfloat16
    dma = pltpu.SemaphoreType.DMA
    tile = math.gcd(seq_count * capacity, 512)
    blocks = chosen_blocks.reshape(-1)
    new_rows = pl.pallas_call(
        functools.partial(kernel, seq_count, section_count),
        out_shape=jax.ShapeDtypeStruct((capacity, width), tokens.dtype),
        in_specs=[vmem] * 3 + [smem] * 2 + [anywhere] * 4,
        out_specs=vmem,
        scratch_shapes=[
            pltpu.VMEM((section_count, 2, capacity, width), bf16),
            pltpu.VMEM((2, slots, BLOCK), jnp.float32),
            pltpu.VMEM((2 * capacity, depth), bf16),
            pltpu.VMEM((depth, kv_cols), bf16),
            pltpu.VMEM((depth, kv_cols), bf16),
            pltpu.VMEM((2, depth, query_cols // 2), bf16),
            pltpu.VMEM((2, w_out.shape[0] * seq_count, w_out.shape[1] // 2), bf16),
            pltpu.VMEM((seq_count * capacity, 2 * kv_cols), bf16),
            pltpu.VMEM((2, query_cols // HEAD_DIM, capacity, HEAD_DIM), bf16),
            pltpu.VMEM((ratio * capacity, HEAD_DIM), jnp.float32),
            pltpu.VMEM((ratio * capacity, 1), jnp.float32),
            pltpu.VMEM((section_count, 2, capacity, query_cols), bf16),
            pltpu.VMEM((2, capacity, width // 2), bf16),
            pltpu.VMEM((2, capacity, width // 2), bf16),
            dma((7, seq_count)),
            dma((2, 7, line)),
            dma((7, line)),
            dma((6,)),
            dma((2, section_count)),
            dma((2, section_count)),
            dma((2, section_count)),
            dma((2, section_count)),
            dma((2,)),
            dma((2,)),
            dma((2,)),
            dma((2,)),
            pltpu.VMEM((seq_count * capacity // tile, tile), jnp.int32),
        ],
        compiler_params=pltpu.CompilerParams(collective_id=0, has_side_effects=True),
    )(
        tokens,
        norm_gain[None, :],
        router_gate.reshape(tok_rows // BLOCK, BLOCK),
        blocks,
        block_counts,
        w_query,
        w_key,
        w_value,
        w_out,
    )
    return pl.pallas_call(
        put,
        out_shape=jax.ShapeDtypeStruct(tokens.shape, tokens.dtype),
        in_specs=[vmem, vmem, smem, smem],
        out_specs=vmem,
    )(tokens, new_rows, blocks, block_counts)


def solution(mesh):
    return jax.shard_map(
        local,
        mesh=mesh,
        in_specs=(
            P("seq", "section"),
            P(),
            P("seq", "section"),
            P("seq", "section"),
            P("seq", "section"),
            P("seq", "section"),
            P("seq"),
            P(),
            P(),
        ),
        out_specs=P("seq", "section"),
        check_vma=False,
    )
```

```python
import functools
import math

import jax
import jax.numpy as jnp
from jax import lax
from jax.experimental import pallas as pl
from jax.experimental.pallas import tpu as pltpu
from jax.sharding import PartitionSpec as P

HEADS = 16
KV_HEADS = 4
HEAD_DIM = 128
BLOCK = 128
EPSILON = 1e-05
MESH = pl.DeviceIdType.MESH

KEY, VALUE, QUERY_A, QUERY_B, OUT_A, OUT_B, PANEL, GUEST_PANEL = range(8)


def repeat(low, high, body):
    if high - low <= 4:
        for step in range(low, high):
            body(step)
    elif high > low:

        def wrapped(step, carry):
            body(step)
            return carry

        lax.fori_loop(low, high, wrapped, 0)


def kernel(
    seq_count,
    section_count,
    tokens_ref,
    gain_ref,
    gate_ref,
    chosen_ref,
    count_ref,
    wq_in,
    wk_in,
    wv_in,
    wo_in,
    out_ref,
    rows_all,
    gate_rows,
    normed_ref,
    wk,
    wv,
    wq,
    wo,
    panel,
    queries_ref,
    numer_ref,
    denom_ref,
    heads_all,
    results,
    returned,
    recv,
    send_line,
    send_pair,
    own_sem,
    rows_send,
    rows_recv,
    heads_send,
    heads_recv,
    guest_send,
    guest_recv,
    back_send,
    back_recv,
    key_slots,
):
    me = lax.axis_index("seq")
    section = lax.axis_index("section")
    line = seq_count // 2
    spot = me // 2
    core = lax.rem(me, 2)
    pair = spot * 2 + 1 - core
    slots = chosen_ref.shape[0] // seq_count
    capacity, width = out_ref.shape
    kv_cols = wk_in.shape[1]
    groups = kv_cols // HEAD_DIM
    ratio = HEADS // KV_HEADS
    half_q = wq_in.shape[1] // 2
    half_o = wo_in.shape[1] // 2
    depth = section_count * width
    first, last = 1, line - 2
    active = (spot >= first) & (spot <= last)
    has_guest = (spot == first) | (spot == last)
    near = jnp.where(spot * 2 < line, 1, -1)
    guest_spot = spot - near
    guest = me - 2 * near
    host = me + 2 * near

    def rows_of(block, size):
        return pl.ds(pl.multiple_of(block * size, size), size)

    def full(chunk, block):
        if chunk == KEY:
            return wk.at[rows_of(block, wk_in.shape[0]), :]
        if chunk == VALUE:
            return wv.at[rows_of(block, wv_in.shape[0]), :]
        if chunk in (QUERY_A, QUERY_B):
            return wq.at[chunk - QUERY_A, rows_of(block, wq_in.shape[0]), :]
        if chunk in (PANEL, GUEST_PANEL):
            return panel.at[rows_of(block, capacity), :]
        return wo.at[chunk - OUT_A, rows_of(block, wo_in.shape[0]), :]

    def own(chunk):
        if chunk == KEY:
            return wk_in
        if chunk == VALUE:
            return wv_in
        if chunk in (QUERY_A, QUERY_B):
            return wq_in.at[:, pl.ds((chunk - QUERY_A) * half_q, half_q)]
        return wo_in.at[:, pl.ds((chunk - OUT_A) * half_o, half_o)]

    def transfer(chunk, block, send_sem, target, mine):
        return pltpu.make_async_remote_copy(
            src_ref=own(chunk) if mine else full(chunk, block),
            dst_ref=full(chunk, block),
            send_sem=send_sem,
            recv_sem=recv.at[min(chunk, PANEL), block],
            device_id={"seq": target},
            device_id_type=MESH,
        )

    def along(chunk, source, sign, mine):
        way = (1 - sign) // 2
        return transfer(
            chunk, source * 2 + core, send_line.at[way, min(chunk, PANEL), source], me + 2 * sign, mine
        )

    def across(chunk, source, mine):
        return transfer(
            chunk, source * 2 + core, send_pair.at[min(chunk, PANEL), source], pair, mine
        )

    def onward(sign):
        return (spot + sign >= first) & (spot + sign <= last)

    def begin(chunk, source):
        mine = chunk < PANEL
        for sign in (1, -1):

            @pl.when(onward(sign))
            def _():
                along(chunk, source, sign, mine).start()

        @pl.when(active)
        def _():
            across(chunk, source, mine).start()

    def relay(chunk, step, sign):
        source = spot - sign * step
        low, high = (first, last) if chunk >= PANEL else (0, line - 1)
        valid = active & (source >= low) & (source <= high)
        if chunk == GUEST_PANEL:
            valid = active & (source == jnp.where(sign > 0, first, last))
            source = source - sign

        @pl.when(valid)
        def _():
            across(chunk, source, False).wait_recv()

            @pl.when(onward(sign))
            def _():
                along(chunk, source, sign, False).start()

            across(chunk, source, False).start()

    def relay_all(chunks, low, high, sides=(1, -1)):
        def body(step):
            for side in sides:
                for chunk in chunks:
                    relay(chunk, step, side * near)

        repeat(low, high, body)

    def await_pair(chunk):
        def body(source):
            transfer(
                chunk, source * 2 + 1 - core, send_pair.at[chunk, source], pair, False
            ).wait_recv()

        repeat(0, line, body)

    def finish_sends(chunk):
        def body(source):
            for sign in (1, -1):
                origin = jnp.clip(source, first, last) if chunk == PANEL else source

                @pl.when(onward(sign) & (origin * sign <= spot * sign))
                def _():
                    along(chunk, source, sign, False).wait_send()

            @pl.when(active)
            def _():
                across(chunk, source, False).wait_send()

        if chunk == PANEL:

            def guarded(source):
                pl.when(active)(lambda: body(source))

            repeat(0, line, guarded)
        else:
            repeat(0, line, body)

    def own_copy(chunk):
        return pltpu.make_async_copy(own(chunk), full(chunk, me), own_sem.at[chunk])

    def spread(buffer, send, receive, who, offset):
        peer = lax.rem(section + offset, section_count)
        return pltpu.make_async_remote_copy(
            src_ref=buffer.at[section, who],
            dst_ref=buffer.at[section, who],
            send_sem=send.at[who, offset],
            recv_sem=receive.at[who, section],
            device_id={"section": peer},
            device_id_type=MESH,
        )

    def await_spread(buffer, send, receive, who):
        for offset in range(1, section_count):
            peer = lax.rem(section + offset, section_count)
            pltpu.make_async_remote_copy(
                src_ref=buffer.at[peer, who],
                dst_ref=buffer.at[peer, who],
                send_sem=send.at[who, offset],
                recv_sem=receive.at[who, peer],
                device_id={"section": peer},
                device_id_type=MESH,
            ).wait_recv()

    def to_host():
        return (
            pltpu.make_async_remote_copy(
                src_ref=rows_all.at[section, 0],
                dst_ref=rows_all.at[section, 1],
                send_sem=guest_send.at[0],
                recv_sem=guest_recv.at[0],
                device_id={"seq": host},
                device_id_type=MESH,
            ),
            pltpu.make_async_remote_copy(
                src_ref=gate_rows.at[0],
                dst_ref=gate_rows.at[1],
                send_sem=guest_send.at[1],
                recv_sem=guest_recv.at[1],
                device_id={"seq": host},
                device_id_type=MESH,
            ),
        )

    def give_back(half, target):
        return pltpu.make_async_remote_copy(
            src_ref=results.at[half],
            dst_ref=returned.at[half],
            send_sem=back_send.at[half],
            recv_sem=back_recv.at[half],
            device_id={"seq": target},
            device_id_type=MESH,
        )

    for slot in range(slots):
        number = chosen_ref[me * slots + slot]
        rows = tokens_ref[:BLOCK, :]
        gates = gate_ref[:1, :]
        for block in range(1, gate_ref.shape[0]):
            rows = jnp.where(
                jnp.full(rows.shape, number, jnp.int32) == block,
                tokens_ref[block * BLOCK : (block + 1) * BLOCK, :],
                rows,
            )
            gates = jnp.where(
                jnp.full(gates.shape, number, jnp.int32) == block,
                gate_ref[block : block + 1, :],
                gates,
            )
        rows_all[section, 0, pl.ds(slot * BLOCK, BLOCK), :] = rows
        gate_rows[0, pl.ds(slot, 1), :] = gates
    total = seq_count * capacity
    tiles, tile = key_slots.shape
    lane = lax.broadcasted_iota(jnp.int32, (1, tile), 1)

    def fill(index):
        key_slot = lane + index * tile
        for piece in range(tile // BLOCK):
            place = index * (tile // BLOCK) + piece
            within = lax.rem(place, slots)
            count = jnp.full((1, tile), count_ref[place // slots], jnp.int32)
            key_slot = jnp.where(
                (lane // BLOCK == piece) & (count <= within), total, key_slot
            )
        key_slots[pl.ds(index, 1), :] = key_slot

    repeat(0, tiles, fill)

    barrier = pltpu.get_barrier_semaphore()

    @pl.when(spot + 1 < line)
    def _():
        pl.semaphore_signal(barrier, inc=1, device_id={"seq": me + 2}, device_id_type=MESH)

    @pl.when(spot > 0)
    def _():
        pl.semaphore_signal(barrier, inc=1, device_id={"seq": me - 2}, device_id_type=MESH)

    pl.semaphore_signal(barrier, inc=1, device_id={"seq": pair}, device_id_type=MESH)
    for offset in range(1, section_count):
        peer = lax.rem(section + offset, section_count)
        pl.semaphore_signal(barrier, inc=1, device_id={"section": peer}, device_id_type=MESH)
    neighbours = jnp.where(spot + 1 < line, 1, 0) + jnp.where(spot > 0, 1, 0)
    pl.semaphore_wait(barrier, section_count + neighbours)

    weights_chunks = (KEY, VALUE, QUERY_A, QUERY_B, OUT_A, OUT_B)

    @pl.when(jnp.logical_not(active))
    def _():
        for copy in to_host():
            copy.start()
        for chunk in weights_chunks:
            begin(chunk, spot)

    def gate_column(who):
        wide = gate_rows[who]
        square = lax.broadcasted_iota(jnp.int32, (BLOCK, BLOCK), 0) == lax.broadcasted_iota(
            jnp.int32, (BLOCK, BLOCK), 1
        )
        return jnp.concatenate(
            [
                jnp.sum(jnp.where(square, wide[slot : slot + 1, :], 0.0), axis=1, keepdims=True)
                for slot in range(slots)
            ],
            axis=0,
        )

    def normalise(who):
        square_sum = jnp.zeros((capacity, 1), jnp.float32)
        for part in range(section_count):
            features = rows_all[part, who].astype(jnp.float32)
            square_sum += jnp.sum(features * features, axis=-1, keepdims=True)
        factor = lax.rsqrt(square_sum / depth + EPSILON)
        for part in range(section_count):
            cols = pl.ds(part * width, width)
            normed_ref[pl.ds(who * capacity, capacity), cols] = (
                rows_all[part, who].astype(jnp.float32) * factor * gain_ref[:, cols]
            ).astype(jnp.bfloat16)

    def attend(who, owner):
        scale = HEAD_DIM ** (-0.5)
        tall = lax.broadcasted_iota(jnp.int32, (ratio * capacity, 1), 0)
        query_slot = lax.rem(tall, capacity) + owner * capacity
        for group in range(groups):
            numer_ref[...] = jnp.zeros_like(numer_ref)
            denom_ref[...] = jnp.zeros_like(denom_ref)

            def fold(index):
                start = index * tile
                key_slot = key_slots[pl.ds(index, 1), :]
                rows = pl.ds(pl.multiple_of(start, tile), tile)
                keys = panel[rows, pl.ds(group * HEAD_DIM, HEAD_DIM)]
                values = panel[rows, pl.ds(kv_cols + group * HEAD_DIM, HEAD_DIM)]
                wide = queries_ref[who, pl.ds(group * ratio, ratio)].reshape(
                    ratio * capacity, HEAD_DIM
                )
                scores = (
                    lax.dot_general(
                        wide, keys, (((1,), (1,)), ((), ())), preferred_element_type=jnp.float32
                    )
                    * scale
                )
                weights = jnp.where(key_slot <= query_slot, jnp.exp(scores), 0.0)
                denom_ref[...] += jnp.sum(weights, axis=-1, keepdims=True)
                numer_ref[...] += jnp.dot(
                    weights.astype(jnp.bfloat16), values, preferred_element_type=jnp.float32
                )

            repeat(0, total // tile, fold)
            safe = jnp.where(denom_ref[...] > 0, denom_ref[...], 1.0)
            result = (numer_ref[...] / safe).astype(jnp.bfloat16)
            for head in range(ratio):
                cols = pl.ds((group * ratio + head) * HEAD_DIM, HEAD_DIM)
                heads_all[section, who, :, cols] = result[head * capacity : (head + 1) * capacity]

    def finish(who, half):
        update = jnp.zeros((capacity, half_o), jnp.float32)
        head_cols = heads_all.shape[3]
        for part in range(section_count):
            update += jnp.dot(
                heads_all[part, who],
                wo[half, pl.ds(part * head_cols, head_cols), :],
                preferred_element_type=jnp.float32,
            )
        cols = pl.ds(half * half_o, half_o)
        return (
            rows_all[section, who, :, cols].astype(jnp.float32) + gate_column(who) * update
        ).astype(out_ref.dtype)

    @pl.when(active)
    def _():
        begin(KEY, spot)
        begin(VALUE, spot)
        for offset in range(1, section_count):
            spread(rows_all, rows_send, rows_recv, 0, offset).start()

        @pl.when(has_guest)
        def _():
            for copy in to_host():
                copy.wait_recv()
            for offset in range(1, section_count):
                spread(rows_all, rows_send, rows_recv, 1, offset).start()

        for chunk in weights_chunks:
            own_copy(chunk).start()
        relay_all((KEY, VALUE), 1, 2, (1,))
        begin(QUERY_A, spot)
        begin(QUERY_B, spot)
        relay_all((KEY, VALUE), 1, 2, (-1,))
        relay_all((KEY, VALUE), 2, line)
        await_spread(rows_all, rows_send, rows_recv, 0)
        normalise(0)
        relay_all((QUERY_A, QUERY_B), 1, 2, (1,))

        @pl.when(has_guest)
        def _():
            await_spread(rows_all, rows_send, rows_recv, 1)
            normalise(1)

        for chunk in (KEY, VALUE):
            await_pair(chunk)
            own_copy(chunk).wait()
        for position, weight in enumerate((wk, wv)):
            sums = jnp.dot(
                normed_ref[...], weight[...], preferred_element_type=jnp.float32
            ).astype(jnp.bfloat16)
            cols = pl.ds(position * kv_cols, kv_cols)
            panel[rows_of(me, capacity), cols] = sums[:capacity]

            @pl.when(has_guest)
            def _():
                panel[rows_of(guest, capacity), cols] = sums[capacity:]

        begin(PANEL, spot)

        @pl.when(has_guest)
        def _():
            begin(GUEST_PANEL, guest_spot)

        begin(OUT_A, spot)
        begin(OUT_B, spot)
        relay_all((QUERY_A, QUERY_B), 1, 2, (-1,))
        relay_all((QUERY_A, QUERY_B), 2, line)
        relay_all((PANEL, GUEST_PANEL), 1, line)
        relay_all((OUT_A, OUT_B), 1, 2, (1,))
        heads_half = half_q // HEAD_DIM
        for half in range(2):
            await_pair(QUERY_A + half)
            own_copy(QUERY_A + half).wait()
            sums = jnp.dot(
                normed_ref[...], wq[half], preferred_element_type=jnp.float32
            ).astype(jnp.bfloat16)
            for who in range(2):
                for head in range(heads_half):
                    queries_ref[who, half * heads_half + head] = sums[
                        who * capacity : (who + 1) * capacity,
                        head * HEAD_DIM : (head + 1) * HEAD_DIM,
                    ]
        await_pair(PANEL)

        @pl.when(has_guest)
        def _():
            attend(1, guest)
            for offset in range(1, section_count):
                spread(heads_all, heads_send, heads_recv, 1, offset).start()

        attend(0, me)
        for offset in range(1, section_count):
            spread(heads_all, heads_send, heads_recv, 0, offset).start()
        for half in range(2):
            relay_all((OUT_A + half,), 1, 2, (-1,))
            relay_all((OUT_A + half,), 2, line)
            await_pair(OUT_A + half)
            own_copy(OUT_A + half).wait()

            @pl.when(has_guest)
            def _():
                if half == 0:
                    await_spread(heads_all, heads_send, heads_recv, 1)
                results[half] = finish(1, half)
                give_back(half, guest).start()

        await_spread(heads_all, heads_send, heads_recv, 0)
        for half in range(2):
            out_ref[:, pl.ds(half * half_o, half_o)] = finish(0, half)
        for offset in range(1, section_count):
            spread(rows_all, rows_send, rows_recv, 0, offset).wait_send()
            spread(heads_all, heads_send, heads_recv, 0, offset).wait_send()

        @pl.when(has_guest)
        def _():
            for offset in range(1, section_count):
                spread(rows_all, rows_send, rows_recv, 1, offset).wait_send()
                spread(heads_all, heads_send, heads_recv, 1, offset).wait_send()
            for half in range(2):
                give_back(half, guest).wait_send()

    for chunk in weights_chunks + (PANEL,):
        finish_sends(chunk)

    @pl.when(jnp.logical_not(active))
    def _():
        for copy in to_host():
            copy.wait_send()
        for half in range(2):
            give_back(half, host).wait_recv()
            out_ref[:, pl.ds(half * half_o, half_o)] = returned[half]


def put(tokens_ref, rows_ref, chosen_ref, count_ref, mixed_ref):
    me = lax.axis_index("seq")
    mixed_ref[...] = tokens_ref[...]
    slots = rows_ref.shape[0] // BLOCK
    for slot in range(slots):

        @pl.when(slot < count_ref[me])
        def _():
            start = pl.multiple_of(chosen_ref[me * slots + slot] * BLOCK, BLOCK)
            mixed_ref[pl.ds(start, BLOCK), :] = rows_ref[slot * BLOCK : (slot + 1) * BLOCK, :]


def local(
    tokens, norm_gain, w_query, w_key, w_value, w_out, router_gate, chosen_blocks, block_counts
):
    seq_count = lax.axis_size("seq")
    section_count = lax.axis_size("section")
    tok_rows, width = tokens.shape
    slots = chosen_blocks.shape[1]
    capacity = slots * BLOCK
    depth = section_count * width
    query_cols = w_query.shape[1]
    kv_cols = w_key.shape[1]
    ratio = HEADS // KV_HEADS
    line = seq_count // 2

    vmem = pl.BlockSpec(memory_space=pltpu.VMEM)
    smem = pl.BlockSpec(memory_space=pltpu.SMEM)
    anywhere = pl.BlockSpec(memory_space=pl.ANY)
    bf16 = jnp.bfloat16
    dma = pltpu.SemaphoreType.DMA
    tile = math.gcd(seq_count * capacity, 512)
    blocks = chosen_blocks.reshape(-1)
    new_rows = pl.pallas_call(
        functools.partial(kernel, seq_count, section_count),
        out_shape=jax.ShapeDtypeStruct((capacity, width), tokens.dtype),
        in_specs=[vmem] * 3 + [smem] * 2 + [anywhere] * 4,
        out_specs=vmem,
        scratch_shapes=[
            pltpu.VMEM((section_count, 2, capacity, width), bf16),
            pltpu.VMEM((2, slots, BLOCK), jnp.float32),
            pltpu.VMEM((2 * capacity, depth), bf16),
            pltpu.VMEM((depth, kv_cols), bf16),
            pltpu.VMEM((depth, kv_cols), bf16),
            pltpu.VMEM((2, depth, query_cols // 2), bf16),
            pltpu.VMEM((2, w_out.shape[0] * seq_count, w_out.shape[1] // 2), bf16),
            pltpu.VMEM((seq_count * capacity, 2 * kv_cols), bf16),
            pltpu.VMEM((2, query_cols // HEAD_DIM, capacity, HEAD_DIM), bf16),
            pltpu.VMEM((ratio * capacity, HEAD_DIM), jnp.float32),
            pltpu.VMEM((ratio * capacity, 1), jnp.float32),
            pltpu.VMEM((section_count, 2, capacity, query_cols), bf16),
            pltpu.VMEM((2, capacity, width // 2), bf16),
            pltpu.VMEM((2, capacity, width // 2), bf16),
            dma((7, seq_count)),
            dma((2, 7, line)),
            dma((7, line)),
            dma((6,)),
            dma((2, section_count)),
            dma((2, section_count)),
            dma((2, section_count)),
            dma((2, section_count)),
            dma((2,)),
            dma((2,)),
            dma((2,)),
            dma((2,)),
            pltpu.VMEM((seq_count * capacity // tile, tile), jnp.int32),
        ],
        compiler_params=pltpu.CompilerParams(collective_id=0, has_side_effects=True),
    )(
        tokens,
        norm_gain[None, :],
        router_gate.reshape(tok_rows // BLOCK, BLOCK),
        blocks,
        block_counts,
        w_query,
        w_key,
        w_value,
        w_out,
    )
    return pl.pallas_call(
        put,
        out_shape=jax.ShapeDtypeStruct(tokens.shape, tokens.dtype),
        in_specs=[vmem, vmem, smem, smem],
        out_specs=vmem,
    )(tokens, new_rows, blocks, block_counts)


def solution(mesh):
    return jax.shard_map(
        local,
        mesh=mesh,
        in_specs=(
            P("seq", "section"),
            P(),
            P("seq", "section"),
            P("seq", "section"),
            P("seq", "section"),
            P("seq", "section"),
            P("seq"),
            P(),
            P(),
        ),
        out_specs=P("seq", "section"),
        check_vma=False,
    )
```

```python
import functools
import math

import jax
import jax.numpy as jnp
from jax import lax
from jax.experimental import pallas as pl
from jax.experimental.pallas import tpu as pltpu
from jax.sharding import PartitionSpec as P

HEADS = 16
KV_HEADS = 4
HEAD_DIM = 128
BLOCK = 128
EPSILON = 1e-05
MESH = pl.DeviceIdType.MESH

KEY, VALUE, QUERY_A, QUERY_B, OUT_A, OUT_B, PANEL, GUEST_PANEL = range(8)


def repeat(low, high, body):
    if high - low <= 4:
        for step in range(low, high):
            body(step)
    elif high > low:

        def wrapped(step, carry):
            body(step)
            return carry

        lax.fori_loop(low, high, wrapped, 0)


def kernel(
    seq_count,
    section_count,
    tokens_ref,
    gain_ref,
    gate_ref,
    chosen_ref,
    count_ref,
    wq_in,
    wk_in,
    wv_in,
    wo_in,
    out_ref,
    rows_all,
    gate_rows,
    normed_ref,
    wk,
    wv,
    wq,
    wo,
    panel,
    queries_ref,
    numer_ref,
    denom_ref,
    heads_all,
    results,
    returned,
    recv,
    send_line,
    send_pair,
    own_sem,
    rows_send,
    rows_recv,
    heads_send,
    heads_recv,
    guest_send,
    guest_recv,
    back_send,
    back_recv,
    key_slots,
):
    me = lax.axis_index("seq")
    section = lax.axis_index("section")
    line = seq_count // 2
    spot = me // 2
    core = lax.rem(me, 2)
    pair = spot * 2 + 1 - core
    slots = chosen_ref.shape[0] // seq_count
    capacity, width = out_ref.shape
    kv_cols = wk_in.shape[1]
    groups = kv_cols // HEAD_DIM
    ratio = HEADS // KV_HEADS
    half_q = wq_in.shape[1] // 2
    half_o = wo_in.shape[1] // 2
    depth = section_count * width
    first, last = 1, line - 2
    active = (spot >= first) & (spot <= last)
    has_guest = (spot == first) | (spot == last)
    near = jnp.where(spot * 2 < line, 1, -1)
    guest_spot = spot - near
    guest = me - 2 * near
    host = me + 2 * near

    def rows_of(block, size):
        return pl.ds(pl.multiple_of(block * size, size), size)

    def full(chunk, block):
        if chunk == KEY:
            return wk.at[rows_of(block, wk_in.shape[0]), :]
        if chunk == VALUE:
            return wv.at[rows_of(block, wv_in.shape[0]), :]
        if chunk in (QUERY_A, QUERY_B):
            return wq.at[chunk - QUERY_A, rows_of(block, wq_in.shape[0]), :]
        if chunk in (PANEL, GUEST_PANEL):
            return panel.at[rows_of(block, capacity), :]
        return wo.at[chunk - OUT_A, rows_of(block, wo_in.shape[0]), :]

    def own(chunk):
        if chunk == KEY:
            return wk_in
        if chunk == VALUE:
            return wv_in
        if chunk in (QUERY_A, QUERY_B):
            return wq_in.at[:, pl.ds((chunk - QUERY_A) * half_q, half_q)]
        return wo_in.at[:, pl.ds((chunk - OUT_A) * half_o, half_o)]

    def transfer(chunk, block, send_sem, target, mine):
        return pltpu.make_async_remote_copy(
            src_ref=own(chunk) if mine else full(chunk, block),
            dst_ref=full(chunk, block),
            send_sem=send_sem,
            recv_sem=recv.at[min(chunk, PANEL), block],
            device_id={"seq": target},
            device_id_type=MESH,
        )

    def along(chunk, source, sign, mine):
        way = (1 - sign) // 2
        return transfer(
            chunk, source * 2 + core, send_line.at[way, min(chunk, PANEL), source], me + 2 * sign, mine
        )

    def across(chunk, source, mine):
        return transfer(
            chunk, source * 2 + core, send_pair.at[min(chunk, PANEL), source], pair, mine
        )

    def onward(sign):
        return (spot + sign >= first) & (spot + sign <= last)

    def begin(chunk, source):
        mine = chunk < PANEL
        for sign in (1, -1):

            @pl.when(onward(sign))
            def _():
                along(chunk, source, sign, mine).start()

        @pl.when(active)
        def _():
            across(chunk, source, mine).start()

    def relay(chunk, step, sign):
        source = spot - sign * step
        low, high = (first, last) if chunk >= PANEL else (0, line - 1)
        valid = active & (source >= low) & (source <= high)
        if chunk == GUEST_PANEL:
            valid = active & (source == jnp.where(sign > 0, first, last))
            source = source - sign

        @pl.when(valid)
        def _():
            across(chunk, source, False).wait_recv()

            @pl.when(onward(sign))
            def _():
                along(chunk, source, sign, False).start()

            across(chunk, source, False).start()

    def relay_all(chunks, low, high, sides=(1, -1)):
        def body(step):
            for side in sides:
                for chunk in chunks:
                    relay(chunk, step, side * near)

        repeat(low, high, body)

    def await_pair(chunk):
        def body(source):
            transfer(
                chunk, source * 2 + 1 - core, send_pair.at[chunk, source], pair, False
            ).wait_recv()

        repeat(0, line, body)

    def finish_sends(chunk):
        def body(source):
            for sign in (1, -1):
                origin = jnp.clip(source, first, last) if chunk == PANEL else source

                @pl.when(onward(sign) & (origin * sign <= spot * sign))
                def _():
                    along(chunk, source, sign, False).wait_send()

            @pl.when(active)
            def _():
                across(chunk, source, False).wait_send()

        if chunk == PANEL:

            def guarded(source):
                pl.when(active)(lambda: body(source))

            repeat(0, line, guarded)
        else:
            repeat(0, line, body)

    def own_copy(chunk):
        return pltpu.make_async_copy(own(chunk), full(chunk, me), own_sem.at[chunk])

    def spread(buffer, send, receive, who, offset):
        peer = lax.rem(section + offset, section_count)
        return pltpu.make_async_remote_copy(
            src_ref=buffer.at[section, who],
            dst_ref=buffer.at[section, who],
            send_sem=send.at[who, offset],
            recv_sem=receive.at[who, section],
            device_id={"section": peer},
            device_id_type=MESH,
        )

    def await_spread(buffer, send, receive, who):
        for offset in range(1, section_count):
            peer = lax.rem(section + offset, section_count)
            pltpu.make_async_remote_copy(
                src_ref=buffer.at[peer, who],
                dst_ref=buffer.at[peer, who],
                send_sem=send.at[who, offset],
                recv_sem=receive.at[who, peer],
                device_id={"section": peer},
                device_id_type=MESH,
            ).wait_recv()

    def to_host():
        return (
            pltpu.make_async_remote_copy(
                src_ref=rows_all.at[section, 0],
                dst_ref=rows_all.at[section, 1],
                send_sem=guest_send.at[0],
                recv_sem=guest_recv.at[0],
                device_id={"seq": host},
                device_id_type=MESH,
            ),
            pltpu.make_async_remote_copy(
                src_ref=gate_rows.at[0],
                dst_ref=gate_rows.at[1],
                send_sem=guest_send.at[1],
                recv_sem=guest_recv.at[1],
                device_id={"seq": host},
                device_id_type=MESH,
            ),
        )

    def give_back(half, target):
        return pltpu.make_async_remote_copy(
            src_ref=results.at[half],
            dst_ref=returned.at[half],
            send_sem=back_send.at[half],
            recv_sem=back_recv.at[half],
            device_id={"seq": target},
            device_id_type=MESH,
        )

    for slot in range(slots):
        number = chosen_ref[me * slots + slot]
        rows = tokens_ref[:BLOCK, :]
        gates = gate_ref[:1, :]
        for block in range(1, gate_ref.shape[0]):
            rows = jnp.where(
                jnp.full(rows.shape, number, jnp.int32) == block,
                tokens_ref[block * BLOCK : (block + 1) * BLOCK, :],
                rows,
            )
            gates = jnp.where(
                jnp.full(gates.shape, number, jnp.int32) == block,
                gate_ref[block : block + 1, :],
                gates,
            )
        rows_all[section, 0, pl.ds(slot * BLOCK, BLOCK), :] = rows
        gate_rows[0, pl.ds(slot, 1), :] = gates
    total = seq_count * capacity
    tiles, tile = key_slots.shape
    lane = lax.broadcasted_iota(jnp.int32, (1, tile), 1)

    def fill(index):
        key_slot = lane + index * tile
        for piece in range(tile // BLOCK):
            place = index * (tile // BLOCK) + piece
            within = lax.rem(place, slots)
            count = jnp.full((1, tile), count_ref[place // slots], jnp.int32)
            key_slot = jnp.where(
                (lane // BLOCK == piece) & (count <= within), total, key_slot
            )
        key_slots[pl.ds(index, 1), :] = key_slot

    repeat(0, tiles, fill)

    barrier = pltpu.get_barrier_semaphore()

    @pl.when(spot + 1 < line)
    def _():
        pl.semaphore_signal(barrier, inc=1, device_id={"seq": me + 2}, device_id_type=MESH)

    @pl.when(spot > 0)
    def _():
        pl.semaphore_signal(barrier, inc=1, device_id={"seq": me - 2}, device_id_type=MESH)

    pl.semaphore_signal(barrier, inc=1, device_id={"seq": pair}, device_id_type=MESH)
    for offset in range(1, section_count):
        peer = lax.rem(section + offset, section_count)
        pl.semaphore_signal(barrier, inc=1, device_id={"section": peer}, device_id_type=MESH)
    neighbours = jnp.where(spot + 1 < line, 1, 0) + jnp.where(spot > 0, 1, 0)
    pl.semaphore_wait(barrier, section_count + neighbours)

    weights_chunks = (KEY, VALUE, QUERY_A, QUERY_B, OUT_A, OUT_B)

    @pl.when(jnp.logical_not(active))
    def _():
        for copy in to_host():
            copy.start()
        for chunk in weights_chunks:
            begin(chunk, spot)

    def gate_column(who):
        wide = gate_rows[who]
        square = lax.broadcasted_iota(jnp.int32, (BLOCK, BLOCK), 0) == lax.broadcasted_iota(
            jnp.int32, (BLOCK, BLOCK), 1
        )
        return jnp.concatenate(
            [
                jnp.sum(jnp.where(square, wide[slot : slot + 1, :], 0.0), axis=1, keepdims=True)
                for slot in range(slots)
            ],
            axis=0,
        )

    def normalise(who):
        square_sum = jnp.zeros((capacity, 1), jnp.float32)
        for part in range(section_count):
            features = rows_all[part, who].astype(jnp.float32)
            square_sum += jnp.sum(features * features, axis=-1, keepdims=True)
        factor = lax.rsqrt(square_sum / depth + EPSILON)
        for part in range(section_count):
            cols = pl.ds(part * width, width)
            normed_ref[pl.ds(who * capacity, capacity), cols] = (
                rows_all[part, who].astype(jnp.float32) * factor * gain_ref[:, cols]
            ).astype(jnp.bfloat16)

    def attend(who, owner):
        scale = HEAD_DIM ** (-0.5)
        tall = lax.broadcasted_iota(jnp.int32, (ratio * capacity, 1), 0)
        query_slot = lax.rem(tall, capacity) + owner * capacity
        for group in range(groups):
            numer_ref[...] = jnp.zeros_like(numer_ref)
            denom_ref[...] = jnp.zeros_like(denom_ref)

            def fold(index):
                start = index * tile
                key_slot = key_slots[pl.ds(index, 1), :]
                rows = pl.ds(pl.multiple_of(start, tile), tile)
                keys = panel[rows, pl.ds(group * HEAD_DIM, HEAD_DIM)]
                values = panel[rows, pl.ds(kv_cols + group * HEAD_DIM, HEAD_DIM)]
                wide = queries_ref[who, pl.ds(group * ratio, ratio)].reshape(
                    ratio * capacity, HEAD_DIM
                )
                scores = (
                    lax.dot_general(
                        wide, keys, (((1,), (1,)), ((), ())), preferred_element_type=jnp.float32
                    )
                    * scale
                )
                weights = jnp.where(key_slot <= query_slot, jnp.exp(scores), 0.0)
                denom_ref[...] += jnp.sum(weights, axis=-1, keepdims=True)
                numer_ref[...] += jnp.dot(
                    weights.astype(jnp.bfloat16), values, preferred_element_type=jnp.float32
                )

            repeat(0, total // tile, fold)
            safe = jnp.where(denom_ref[...] > 0, denom_ref[...], 1.0)
            result = (numer_ref[...] / safe).astype(jnp.bfloat16)
            for head in range(ratio):
                cols = pl.ds((group * ratio + head) * HEAD_DIM, HEAD_DIM)
                heads_all[section, who, :, cols] = result[head * capacity : (head + 1) * capacity]

    def finish(who, half):
        update = jnp.zeros((capacity, half_o), jnp.float32)
        head_cols = heads_all.shape[3]
        for part in range(section_count):
            update += jnp.dot(
                heads_all[part, who],
                wo[half, pl.ds(part * head_cols, head_cols), :],
                preferred_element_type=jnp.float32,
            )
        cols = pl.ds(half * half_o, half_o)
        return (
            rows_all[section, who, :, cols].astype(jnp.float32) + gate_column(who) * update
        ).astype(out_ref.dtype)

    @pl.when(active)
    def _():
        begin(KEY, spot)
        begin(VALUE, spot)
        for offset in range(1, section_count):
            spread(rows_all, rows_send, rows_recv, 0, offset).start()

        @pl.when(has_guest)
        def _():
            for copy in to_host():
                copy.wait_recv()
            for offset in range(1, section_count):
                spread(rows_all, rows_send, rows_recv, 1, offset).start()

        for chunk in weights_chunks:
            own_copy(chunk).start()
        relay_all((KEY, VALUE), 1, 2, (1,))
        begin(QUERY_A, spot)
        begin(QUERY_B, spot)
        relay_all((KEY, VALUE), 1, 2, (-1,))
        relay_all((KEY, VALUE), 2, line)
        await_spread(rows_all, rows_send, rows_recv, 0)
        normalise(0)
        relay_all((QUERY_A, QUERY_B), 1, 2, (1,))

        @pl.when(has_guest)
        def _():
            await_spread(rows_all, rows_send, rows_recv, 1)
            normalise(1)

        for chunk in (KEY, VALUE):
            await_pair(chunk)
            own_copy(chunk).wait()
        for position, weight in enumerate((wk, wv)):
            sums = jnp.dot(
                normed_ref[...], weight[...], preferred_element_type=jnp.float32
            ).astype(jnp.bfloat16)
            cols = pl.ds(position * kv_cols, kv_cols)
            panel[rows_of(me, capacity), cols] = sums[:capacity]

            @pl.when(has_guest)
            def _():
                panel[rows_of(guest, capacity), cols] = sums[capacity:]

        begin(PANEL, spot)

        @pl.when(has_guest)
        def _():
            begin(GUEST_PANEL, guest_spot)

        begin(OUT_A, spot)
        begin(OUT_B, spot)
        relay_all((QUERY_A, QUERY_B), 1, 2, (-1,))
        relay_all((QUERY_A, QUERY_B), 2, line)
        relay_all((PANEL, GUEST_PANEL), 1, line)
        relay_all((OUT_A, OUT_B), 1, 2, (1,))
        heads_half = half_q // HEAD_DIM
        for half in range(2):
            await_pair(QUERY_A + half)
            own_copy(QUERY_A + half).wait()
            sums = jnp.dot(
                normed_ref[...], wq[half], preferred_element_type=jnp.float32
            ).astype(jnp.bfloat16)
            for who in range(2):
                for head in range(heads_half):
                    queries_ref[who, half * heads_half + head] = sums[
                        who * capacity : (who + 1) * capacity,
                        head * HEAD_DIM : (head + 1) * HEAD_DIM,
                    ]
        await_pair(PANEL)

        @pl.when(has_guest)
        def _():
            attend(1, guest)
            for offset in range(1, section_count):
                spread(heads_all, heads_send, heads_recv, 1, offset).start()

        attend(0, me)
        for offset in range(1, section_count):
            spread(heads_all, heads_send, heads_recv, 0, offset).start()
        relay_all((OUT_A, OUT_B), 1, 2, (-1,))
        relay_all((OUT_A, OUT_B), 2, line)
        for half in range(2):
            await_pair(OUT_A + half)
            own_copy(OUT_A + half).wait()

        @pl.when(has_guest)
        def _():
            await_spread(heads_all, heads_send, heads_recv, 1)
            for half in range(2):
                results[half] = finish(1, half)
                give_back(half, guest).start()

        await_spread(heads_all, heads_send, heads_recv, 0)
        for half in range(2):
            out_ref[:, pl.ds(half * half_o, half_o)] = finish(0, half)
        for offset in range(1, section_count):
            spread(rows_all, rows_send, rows_recv, 0, offset).wait_send()
            spread(heads_all, heads_send, heads_recv, 0, offset).wait_send()

        @pl.when(has_guest)
        def _():
            for offset in range(1, section_count):
                spread(rows_all, rows_send, rows_recv, 1, offset).wait_send()
                spread(heads_all, heads_send, heads_recv, 1, offset).wait_send()
            for half in range(2):
                give_back(half, guest).wait_send()

    for chunk in weights_chunks + (PANEL,):
        finish_sends(chunk)

    @pl.when(jnp.logical_not(active))
    def _():
        for copy in to_host():
            copy.wait_send()
        for half in range(2):
            give_back(half, host).wait_recv()
            out_ref[:, pl.ds(half * half_o, half_o)] = returned[half]


def put(tokens_ref, rows_ref, chosen_ref, count_ref, mixed_ref):
    me = lax.axis_index("seq")
    mixed_ref[...] = tokens_ref[...]
    slots = rows_ref.shape[0] // BLOCK
    for slot in range(slots):

        @pl.when((slot < count_ref[me]) & (chosen_ref[me * slots + slot] == pl.program_id(0)))
        def _():
            mixed_ref[...] = rows_ref[slot * BLOCK : (slot + 1) * BLOCK, :]


def local(
    tokens, norm_gain, w_query, w_key, w_value, w_out, router_gate, chosen_blocks, block_counts
):
    seq_count = lax.axis_size("seq")
    section_count = lax.axis_size("section")
    tok_rows, width = tokens.shape
    slots = chosen_blocks.shape[1]
    capacity = slots * BLOCK
    depth = section_count * width
    query_cols = w_query.shape[1]
    kv_cols = w_key.shape[1]
    ratio = HEADS // KV_HEADS
    line = seq_count // 2

    vmem = pl.BlockSpec(memory_space=pltpu.VMEM)
    smem = pl.BlockSpec(memory_space=pltpu.SMEM)
    anywhere = pl.BlockSpec(memory_space=pl.ANY)
    bf16 = jnp.bfloat16
    dma = pltpu.SemaphoreType.DMA
    tile = math.gcd(seq_count * capacity, 512)
    blocks = chosen_blocks.reshape(-1)
    new_rows = pl.pallas_call(
        functools.partial(kernel, seq_count, section_count),
        out_shape=jax.ShapeDtypeStruct((capacity, width), tokens.dtype),
        in_specs=[vmem] * 3 + [smem] * 2 + [anywhere] * 4,
        out_specs=vmem,
        scratch_shapes=[
            pltpu.VMEM((section_count, 2, capacity, width), bf16),
            pltpu.VMEM((2, slots, BLOCK), jnp.float32),
            pltpu.VMEM((2 * capacity, depth), bf16),
            pltpu.VMEM((depth, kv_cols), bf16),
            pltpu.VMEM((depth, kv_cols), bf16),
            pltpu.VMEM((2, depth, query_cols // 2), bf16),
            pltpu.VMEM((2, w_out.shape[0] * seq_count, w_out.shape[1] // 2), bf16),
            pltpu.VMEM((seq_count * capacity, 2 * kv_cols), bf16),
            pltpu.VMEM((2, query_cols // HEAD_DIM, capacity, HEAD_DIM), bf16),
            pltpu.VMEM((ratio * capacity, HEAD_DIM), jnp.float32),
            pltpu.VMEM((ratio * capacity, 1), jnp.float32),
            pltpu.VMEM((section_count, 2, capacity, query_cols), bf16),
            pltpu.VMEM((2, capacity, width // 2), bf16),
            pltpu.VMEM((2, capacity, width // 2), bf16),
            dma((7, seq_count)),
            dma((2, 7, line)),
            dma((7, line)),
            dma((6,)),
            dma((2, section_count)),
            dma((2, section_count)),
            dma((2, section_count)),
            dma((2, section_count)),
            dma((2,)),
            dma((2,)),
            dma((2,)),
            dma((2,)),
            pltpu.VMEM((seq_count * capacity // tile, tile), jnp.int32),
        ],
        compiler_params=pltpu.CompilerParams(collective_id=0, has_side_effects=True),
    )(
        tokens,
        norm_gain[None, :],
        router_gate.reshape(tok_rows // BLOCK, BLOCK),
        blocks,
        block_counts,
        w_query,
        w_key,
        w_value,
        w_out,
    )
    return pl.pallas_call(
        put,
        out_shape=jax.ShapeDtypeStruct(tokens.shape, tokens.dtype),
        grid=(tok_rows // BLOCK,),
        in_specs=[pl.BlockSpec((BLOCK, width), lambda step: (step, 0)), vmem, smem, smem],
        out_specs=pl.BlockSpec((BLOCK, width), lambda step: (step, 0)),
    )(tokens, new_rows, blocks, block_counts)


def solution(mesh):
    return jax.shard_map(
        local,
        mesh=mesh,
        in_specs=(
            P("seq", "section"),
            P(),
            P("seq", "section"),
            P("seq", "section"),
            P("seq", "section"),
            P("seq", "section"),
            P("seq"),
            P(),
            P(),
        ),
        out_specs=P("seq", "section"),
        check_vma=False,
    )
```
